512 devices in a mesh: seq: 64 (over x, z, y_hi), head: 8 (over y_lo, core).
Axes of the slice: x: 4, y: 8 (y_hi: 2, y_lo: 4; y = y_hi * 4 + y_lo), z: 8, core: 2. Of those that a mesh axis runs over, the one named last changes fastest.
Arguments:
- layer_input: bfloat16 [8192, 4096], P('seq', 'head'), may hold values from -16 to 16
- query_rows: bfloat16 [8192, 2048], P('seq', 'head'), may hold values from -6 to 6
- key_matrix_rows: bfloat16 [8192, 2048], P('seq', 'head'), may hold values from -1.25 to 1.25
- value_rows: bfloat16 [8192, 2048], P('seq', 'head'), may hold values from -6 to 6
- beta_rows: float32 [8192, 16], P('seq', 'head'), may hold values from 0 to 0.9, as said below
- log_gate: float32 [8192, 16], P('seq', 'head'), may hold values from -1.3 to 0, as said below
- grad_out: bfloat16 [8192, 2048], P('seq', 'head'), may hold values from -6 to 6
Outputs:
- grad_query: bfloat16 [8192, 2048], P('seq', 'head')
- grad_key: bfloat16 [8192, 2048], P('seq', 'head')
- grad_value: bfloat16 [8192, 2048], P('seq', 'head')
- grad_beta: float32 [8192, 16], P('seq', 'head')
- grad_log_gate: float32 [8192, 16], P('seq', 'head')
- grad_weight: bfloat16 [4096, 2048], P(None, 'head')
The draws below stay inside these ranges and needn't reach their ends.
Inputs may be any that keep to these rules, and one draw needn't show every extreme that they name: `beta_rows`: write strengths vary from token to token and from head to head. `log_gate`: decay rates vary from token to token and from head to head.
All inputs are finite; a program needn't handle non-finite values.
Results may differ from the reference program's by a relative error of at most 0.0049.
Values may be sent and summed in bfloat16 or wider, within the bound.
A program may use at most 128 MiB of HBM per device.

```python
import jax
import jax.numpy as jnp
from jax import lax

D = 4096
HEADS = 16
HD = 128
BLOCK = 64
TOK_DEV = 128
TOKENS = 8192


def head_kinds(key):
    picks = jax.random.randint(jax.random.fold_in(key, 11), (HEADS,), 0, 2)
    return picks.astype(jnp.float32)


def log_uniform(key, shape, lower_end, upper_end):
    return jnp.exp(jax.random.uniform(key, shape, jnp.float32, jnp.log(lower_end), jnp.log(upper_end)))


def draw_beta_rows(key, part):
    fast = head_kinds(key)
    fast_part = jax.random.uniform(jax.random.fold_in(key, 31), (TOKENS, HEADS), jnp.float32, 0.2, 0.9)
    slow_part = log_uniform(jax.random.fold_in(key, 32), (TOKENS, HEADS), 0.15 * HD / TOKENS, 0.45 * HD / TOKENS)
    return jnp.where(fast[None, :] > 0.5, fast_part, slow_part).astype(jnp.float32)


def draw_log_gate(key, part):
    fast = head_kinds(key)
    slow_rate = log_uniform(jax.random.fold_in(key, 21), (TOKENS, HEADS), 0.1 / TOKENS, 0.3 / TOKENS)
    fast_rate = log_uniform(jax.random.fold_in(key, 22), (TOKENS, HEADS), 1.0 / 50.0, 1.0 / 30.0)
    fading_velocity = jnp.where(fast[None, :] > 0.5, fast_rate, slow_rate)
    blocks = log_uniform(jax.random.fold_in(key, 23), (TOKENS // TOK_DEV, HEADS), 0.5, 2.0)
    fading_velocity = fading_velocity * jnp.repeat(blocks, TOK_DEV, axis=0)
    element_slots = jax.random.randint(jax.random.fold_in(key, 24), (2, HEADS), 0, TOKENS)
    fading_losses = jnp.log(jax.random.uniform(jax.random.fold_in(key, 25), (2, HEADS), jnp.float32, 0.55, 0.8))
    element_offsets = jnp.arange(TOKENS)[:, None, None]
    spike_clusters = jnp.where(element_offsets == element_slots[None], fading_losses[None], 0.0).sum(axis=1)
    return (spike_clusters - fading_velocity).astype(jnp.float32)


def raised(array, rng, source, target, shards_of, factor):
    owner, partner = [(jnp.arange(array.shape[position]) // (array.shape[position] // shards_of)).reshape([-1 if axis == position else 1 for axis in range(array.ndim)]) for position in (source, target)]
    chosen = jax.random.permutation(rng, shards_of)[partner]
    strong = (owner == chosen) | (owner == (partner + shards_of // 2) % shards_of)
    return jnp.where(strong, factor * array, array)


def steps_of(rng, dims, cuts, low, top_value):
    def one(dim, parts):
        heights = jax.random.uniform(jax.random.fold_in(jax.random.fold_in(rng, 6), dim), (parts,), jnp.float32, low / len(cuts), top_value / len(cuts))
        return jnp.repeat(jnp.exp(heights), dims[dim] // parts).reshape((-1,) + (1,) * (len(dims) - dim - 1))

    level = one(*cuts[0])
    for cut in cuts[1:]:
        level = level * one(*cut)
    return level


def noise(stream_key, dims, deviation, most, cuts=(), kind=jnp.bfloat16):
    factor_of = steps_of(stream_key, dims, cuts, -0.22, 0.18) if cuts else 1.0
    values = jax.random.normal(stream_key, dims, jnp.float32) * deviation * factor_of
    return jnp.minimum(jnp.maximum(values, -most), most).astype(kind)


def gaussian_with(key, extent, scale, reach, shards, heavy, kind=jnp.bfloat16):
    entries = scale * jax.random.normal(key, extent, jnp.float32)
    if shards:
        entries = entries * steps_of(key, extent, shards, -0.22, 0.18)
    return jnp.clip(raised(entries, jax.random.fold_in(key, 3), *heavy), -reach, reach).astype(kind)


def setup_inputs(seed: int = 0) -> dict:
    streams_of = jax.random.split(jax.random.key(seed), 8)
    layer_input = gaussian_with(streams_of[0], (TOKENS, D), 1.0, 16.0, ((0, 64), (1, 8)), (0, 1, 64, 4.0))
    query_rows = noise(streams_of[1], (TOKENS, HEADS * HD), 1.0, 6.0, ((0, 64), (1, 8)))
    key_matrix_rows = noise(streams_of[2], (TOKENS, HEADS * HD), 0.088, 1.25, ((0, 64), (1, 8)))
    value_rows = noise(streams_of[3], (TOKENS, HEADS * HD), 1.0, 6.0, ((0, 64), (1, 8)))
    beta_rows = draw_beta_rows(jax.random.fold_in(streams_of[7], 71), 0)
    log_gate = draw_log_gate(jax.random.fold_in(streams_of[7], 71), 0)
    grad_out = noise(streams_of[6], (TOKENS, HEADS * HD), 1.0, 6.0, ((0, 64), (1, 8)))
    return dict(layer_input=layer_input, query_rows=query_rows, key_matrix_rows=key_matrix_rows, value_rows=value_rows, beta_rows=beta_rows, log_gate=log_gate, grad_out=grad_out)


HIGHEST_PRECISION = lax.Precision.HIGHEST

def product(left_side, right_side):
    return jnp.matmul(left_side, right_side, precision=HIGHEST_PRECISION)

def flipped(matrix):
    return jnp.swapaxes(matrix, -1, -2)

def unit_inverse(strict_lower):
    order_size = strict_lower.shape[-1]
    identity = jnp.eye(order_size, dtype=strict_lower.dtype)
    result = identity - strict_lower
    exponent_summand = strict_lower
    covered = 2
    while covered < order_size:
        exponent_summand = product(exponent_summand, exponent_summand)
        result = product(result, identity + exponent_summand)
        covered = covered * 2
    return result

def block_parts(key_block, strength, log_decay):
    order_size = log_decay.shape[-1]
    running = jnp.cumsum(log_decay, axis=-1)
    line_number = lax.broadcasted_iota(jnp.int32, (order_size, order_size), 0)
    col_index = lax.broadcasted_iota(jnp.int32, (order_size, order_size), 1)
    causal = line_number >= col_index
    strict = line_number > col_index
    spread = running[..., :, None] - running[..., None, :]
    decay_table = jnp.where(causal, jnp.exp(jnp.where(causal, spread, 0.0)), 0.0)
    strict_lower = jnp.where(strict, strength[..., :, None] * decay_table * product(key_block, flipped(key_block)), 0.0)
    growth = jnp.exp(running)
    tail_decay = jnp.exp(running[..., -1:] - running)
    return (decay_table, growth, tail_decay, unit_inverse(strict_lower))

def segment(query_block, key_block, value_block, strength, log_decay, init_state, with_out):
    decay_table, growth, tail_decay, inverse = block_parts(key_block, strength, log_decay)
    pseudo = product(inverse, strength[..., None] * value_block)
    erasure = product(inverse, (strength * growth)[..., None] * key_block)
    written = flipped(tail_decay[..., None] * key_block)
    keep_all = growth[..., -1]
    argument_sequence = [pseudo, erasure, written, keep_all]
    if with_out:
        argument_sequence = argument_sequence + [decay_table * product(query_block, flipped(key_block)), growth[..., None] * query_block]

    def advance(carry_state, pieces):
        update = pieces[0] - product(pieces[1], carry_state)
        after_state = pieces[3] * carry_state + product(pieces[2], update)
        if with_out:
            return (after_state, product(pieces[5], carry_state) + product(pieces[4], update))
        return (after_state, None)
    return lax.scan(advance, init_state, tuple(argument_sequence))

def head_grads(pieces):
    query_head, key_head, value_head, strength_head, decay_head, grad_head = pieces
    block_count = TOKENS // BLOCK

    def forward(query_all, key_all, value_all, strength_all, decay_all):
        zero_state = jnp.zeros((HD, HD), jnp.float32)
        final_state, outputs = segment(query_all.reshape(block_count, BLOCK, HD), key_all.reshape(block_count, BLOCK, HD), value_all.reshape(block_count, BLOCK, HD), strength_all.reshape(block_count, BLOCK), decay_all.reshape(block_count, BLOCK), zero_state, True)
        return outputs.reshape(TOKENS, HD)
    outputs, pull_back = jax.vjp(forward, query_head.astype(jnp.float32), key_head.astype(jnp.float32), value_head.astype(jnp.float32), strength_head, decay_head)
    return pull_back(grad_head.astype(jnp.float32))

def reference(layer_input, query_rows, key_matrix_rows, value_rows, beta_rows, log_gate, grad_out):

    def per_head_apply(matrix):
        return matrix.reshape(TOKENS, HEADS, HD).transpose(1, 0, 2)

    def to_rows(tensor):
        return tensor.transpose(1, 0, 2).reshape(TOKENS, HEADS * HD).astype(jnp.bfloat16)
    gradients = lax.map(head_grads, (per_head_apply(query_rows), per_head_apply(key_matrix_rows), per_head_apply(value_rows), beta_rows.T, log_gate.T, per_head_apply(grad_out)))
    grad_value = to_rows(gradients[2])
    grad_weight = jnp.dot(layer_input.T, grad_value, preferred_element_type=jnp.float32).astype(jnp.bfloat16)
    return (to_rows(gradients[0]), to_rows(gradients[1]), grad_value, gradients[3].T, gradients[4].T, grad_weight)
```

```python
import jax
import jax.numpy as jnp
from jax import lax
from jax.experimental import pallas as pl
from jax.experimental.pallas import tpu as pltpu
from jax.sharding import PartitionSpec as P

HD = 128
T = 128
F32 = jnp.float32
BF16 = jnp.bfloat16
HIGHEST = lax.Precision.HIGHEST
NY = 2


def dot(a, b, ca=1, cb=0):
    return lax.dot_general(
        a, b, (((ca,), (cb,)), ((), ())), precision=HIGHEST, preferred_element_type=F32
    )


def dot_exact(a, b, ca=1, cb=0):
    return lax.dot_general(a, b, (((ca,), (cb,)), ((), ())), preferred_element_type=F32)


def iotas():
    return (
        lax.broadcasted_iota(jnp.int32, (T, T), 0),
        lax.broadcasted_iota(jnp.int32, (T, T), 1),
    )


def unit_inverse(strict_lower):
    line, col = iotas()
    same = (line >= 64) == (col >= 64)
    diag_part = jnp.where(same, strict_lower, 0.0)
    below = jnp.where(same, 0.0, strict_lower)
    inverse = jnp.where(line == col, 1.0, 0.0) - diag_part
    power = dot(diag_part, diag_part)
    covered = 4
    while covered < 64:
        both = dot(jnp.concatenate([power, inverse], 0), power)
        inverse = inverse + both[T:]
        power = both[:T]
        covered = covered * 2
    inverse = inverse + dot(inverse, power)
    return inverse - dot(dot(inverse, below), inverse)


def gate_parts(lg):
    line, col = iotas()
    lg_row = jnp.sum(jnp.where(line == col, lg, 0.0), axis=0, keepdims=True)
    run_col = jnp.sum(jnp.where(col <= line, lg_row, 0.0), axis=1, keepdims=True)
    run_row = jnp.sum(jnp.where(line <= col, lg, 0.0), axis=0, keepdims=True)
    total = jnp.sum(lg, axis=0, keepdims=True)
    causal = line >= col
    decay = jnp.where(causal, jnp.exp(jnp.where(causal, run_col - run_row, 0.0)), 0.0)
    return decay, jnp.exp(run_col), jnp.exp(total - run_col), jnp.exp(total)


def local_maps(q, k, v, do, beta, lg):
    line, col = iotas()
    decay, growth, tail, keep = gate_parts(lg)
    keys = k.astype(F32)
    scores = decay * dot_exact(q, k, 1, 1)
    lower = beta * jnp.where(line > col, decay * dot_exact(k, k, 1, 1), 0.0)
    inverse = unit_inverse(lower)
    uw = dot(inverse, jnp.concatenate([beta * v.astype(F32), (beta * growth) * keys], 1))
    back = dot(scores, do.astype(F32), 0, 0)
    bw = dot(tail * keys, uw, 0, 0)
    eye = jnp.where(line == col, 1.0, 0.0)
    a = keep * eye - bw[:, HD:]
    b = bw[:, :HD]
    c = dot(growth * q.astype(F32), do.astype(F32), 0, 0) - dot(uw[:, HD:], back, 0, 0)
    return (a, b, c), (inverse, uw, back)


def local_grads(q, k, v, do, beta, lg, inverse, uw, back, state, adj):
    line, col = iotas()
    decay, growth, tail, keep = gate_parts(lg)
    queries, keys, values, grads = (m.astype(F32) for m in (q, k, v, do))
    update = uw[:, :HD] - dot(uw[:, HD:], state)
    d_update = back + dot(tail * keys, adj)
    e = dot(inverse, d_update, 0, 0)
    de = jnp.concatenate([grads, e], 0)
    by_state = dot(de, state, 1, 1)
    by_update = dot(de, update, 1, 1)
    nz = dot(update, adj, 1, 1)
    y = decay * by_update[:T]
    xp = -jnp.where(line > col, decay * by_update[T:], 0.0)
    by_key = dot(jnp.concatenate([xp, y], 0), keys)
    r = by_key[:T] - growth * by_state[T:]
    crossed = dot(
        jnp.concatenate([beta * xp, y], 0), jnp.concatenate([keys, queries], 0), 0, 0
    )
    dq = growth * by_state[:T] + by_key[T:]
    tail_nz = tail * nz
    dk_col = crossed + tail_nz
    dk_row = beta * r
    dv = beta * e
    d_beta = jnp.sum(e * values + keys * r, axis=1, keepdims=True)
    d_run = jnp.sum(queries * dq + keys * (dk_row - dk_col), axis=1, keepdims=True)
    last = jnp.sum(tail_nz * keys, axis=(0, 1), keepdims=True) + keep * jnp.sum(
        adj * state, axis=(0, 1), keepdims=True
    )
    d_run_row = jnp.sum(jnp.where(line == col, d_run, 0.0), axis=0, keepdims=True)
    d_lg = jnp.sum(jnp.where(col >= line, d_run_row, 0.0), axis=1, keepdims=True) + last
    return dq, dk_row + dk_col, dv, d_beta, d_lg


def head_of(ref, h):
    return ref[:, h * HD : (h + 1) * HD]


def maps_kernel(q, k, v, do, beta, lg, maps, inverse, uw, back):
    for h in range(2):
        (a, b, c), (inv, u, f) = local_maps(
            head_of(q, h), head_of(k, h), head_of(v, h), head_of(do, h),
            beta[:, h : h + 1], lg[:, h : h + 1],
        )
        maps[h, 0:HD] = a
        maps[h, HD : 2 * HD] = b
        maps[h, 2 * HD : 3 * HD] = c
        inverse[h] = inv
        uw[h] = u
        back[h] = f


def grads_kernel(q, k, v, do, beta, lg, inverse, uw, back, sz, dq, dk, dv, d_beta, d_lg):
    betas, lgs = [], []
    for h in range(2):
        gq, gk, gv, gb, gl = local_grads(
            head_of(q, h), head_of(k, h), head_of(v, h), head_of(do, h),
            beta[:, h : h + 1], lg[:, h : h + 1],
            inverse[h], uw[h], back[h], sz[h, 0:HD], sz[h, HD : 2 * HD],
        )
        dq[:, h * HD : (h + 1) * HD] = gq.astype(BF16)
        dk[:, h * HD : (h + 1) * HD] = gk.astype(BF16)
        dv[:, h * HD : (h + 1) * HD] = gv.astype(BF16)
        betas.append(gb)
        lgs.append(gl)
    d_beta[...] = jnp.concatenate(betas, 1)
    d_lg[...] = jnp.concatenate(lgs, 1)


class Place:
    def __init__(self, nx, nz):
        s = lax.axis_index("seq")
        self.nx, self.nz = nx, nz
        self.x = s // (nz * NY)
        self.z = lax.rem(s // NY, nz)
        self.y = lax.rem(s, NY)

    def at(self, x=None, z=None, y=None):
        x = self.x if x is None else x
        z = self.z if z is None else z
        y = self.y if y is None else y
        return {"seq": (x * self.nz + z) * NY + y}

    def right(self):
        return self.at(z=lax.rem(self.z + 1, self.nz))

    def left(self):
        return self.at(z=lax.rem(self.z + self.nz - 1, self.nz))

    def partner(self):
        return self.at(y=1 - self.y)

    def other_x(self, t):
        return lax.rem(self.x + t, self.nx)

    def greet(self):
        barrier = pltpu.get_barrier_semaphore()
        peers = [self.partner(), self.right(), self.left()]
        peers += [self.at(x=self.other_x(t)) for t in range(1, self.nx)]
        for peer in peers:
            pl.semaphore_signal(
                barrier, inc=1, device_id=peer, device_id_type=pl.DeviceIdType.MESH
            )
        pl.semaphore_wait(barrier, len(peers))


def remote(src, dst, send, recv, device):
    return pltpu.make_async_remote_copy(
        src_ref=src, dst_ref=dst, send_sem=send, recv_sem=recv,
        device_id=device, device_id_type=pl.DeviceIdType.MESH,
    )


def ring_z(place, view, rows, ssem, rsem):
    nz, z = place.nz, place.z
    steps = nz // 2
    sent = []
    before = [None, None]
    for t in range(1, steps + 1):
        start, count = (0, rows) if t < steps else (0, rows // 2)
        src = view(lax.rem(z + nz - t + 1, nz), start, count)
        if before[0] is not None:
            before[0].wait_recv()
        before[0] = remote(src, src, ssem.at[0, t - 1], rsem.at[0, t - 1], place.right())
        before[0].start()
        start, count = (0, rows) if t < steps else (rows // 2, rows // 2)
        src = view(lax.rem(z + t - 1, nz), start, count)
        if before[1] is not None:
            before[1].wait_recv()
        before[1] = remote(src, src, ssem.at[1, t - 1], rsem.at[1, t - 1], place.left())
        before[1].start()
        sent += before
    before[0].wait_recv()
    before[1].wait_recv()
    for copy in sent:
        copy.wait_send()


def chains(blocks, count, forth, aback):
    width = forth.shape[2] - HD

    def step(n, carry):
        m = count - 1 - n
        new = dot(blocks[n, 0:HD], forth[n])
        old = dot(blocks[m, 0:HD], aback[m + 1], 0, 0)
        if width:
            forth[n + 1, :, 0:width] = new[:, :width]
            aback[m, :, 0:width] = old[:, :width]
        forth[n + 1, :, width:] = new[:, width:] + blocks[n, HD : 2 * HD]
        aback[m, :, width:] = old[:, width:] + blocks[m, 2 * HD : 3 * HD]
        return carry

    lax.fori_loop(0, count, step, 0)


def scan_kernel(
    nx, nz, maps, sz, pair, zbuf, xbuf, zf, zb, xf, xb, both, s1, r1, zs, zr, xs, xr, s2, r2
):
    place = Place(nx, nz)
    x, z, y = place.x, place.z, place.y
    place.greet()
    first = remote(maps.at[1 - y], pair.at[y], s1, r1, place.partner())
    first.start()
    pair[y] = maps[y]
    line, col = iotas()
    eye = jnp.where(line == col, 1.0, 0.0)
    zero = jnp.zeros((HD, HD), F32)
    for ref, slot in ((zf, 0), (zb, nz)):
        ref[slot, :, 0:HD] = eye
        ref[slot, :, HD:] = zero
    xf[0] = zero
    xb[nx] = zero
    first.wait_recv()
    a0, a1 = pair[0, 0:HD], pair[1, 0:HD]
    ab = dot(a1, jnp.concatenate([a0, pair[0, HD : 2 * HD]], 1))
    zbuf[z, 0:HD] = ab[:, :HD]
    zbuf[z, HD : 2 * HD] = ab[:, HD:] + pair[1, HD : 2 * HD]
    zbuf[z, 2 * HD : 3 * HD] = pair[0, 2 * HD : 3 * HD] + dot(a0, pair[1, 2 * HD : 3 * HD], 0, 0)
    ring_z(place, lambda slot, start, count: zbuf.at[slot, pl.ds(start, count)], 3 * HD, zs, zr)
    chains(zbuf, nz, zf, zb)
    xbuf[x, 0:HD] = zf[nz, :, 0:HD]
    xbuf[x, HD : 2 * HD] = zf[nz, :, HD:]
    xbuf[x, 2 * HD : 3 * HD] = zb[0, :, HD:]
    copies = []
    for t in range(1, nx):
        copy = remote(
            xbuf.at[x], xbuf.at[x], xs.at[t - 1], xr.at[t - 1], place.at(x=place.other_x(t))
        )
        copy.start()
        copies.append(copy)
    for copy in copies:
        copy.wait_recv()
    chains(xbuf, nx, xf, xb)
    state = dot(zf[z, :, 0:HD], xf[x]) + zf[z, :, HD:]
    adj = dot(zb[z + 1, :, 0:HD], xb[x + 1]) + zb[z + 1, :, HD:]
    both[0, 0:HD] = state
    both[0, HD : 2 * HD] = dot(pair[1, 0:HD], adj, 0, 0) + pair[1, 2 * HD : 3 * HD]
    both[1, 0:HD] = dot(pair[0, 0:HD], state) + pair[0, HD : 2 * HD]
    both[1, HD : 2 * HD] = adj
    last = remote(both.at[1 - y], sz.at[y], s2, r2, place.partner())
    last.start()
    sz[y] = both[y]
    first.wait_send()
    for copy in copies:
        copy.wait_send()
    last.wait()


def weight_kernel(nx, nz, gv, xg, out, gbuf, psend, precv, ybuf, gs, gr, ps, pr, ys, yr, as_, ar, zs, zr):
    place = Place(nx, nz)
    x, z, y = place.x, place.z, place.y
    place.greet()
    gbuf[z] = gv[...]
    ring_z(place, lambda slot, start, count: gbuf.at[slot, pl.ds(start, count)], T, gs, gr)
    feats = xg.shape[1]
    piece = feats // nx
    cols = gv.shape[1]
    for n in range(nx):
        total = dot_exact(
            xg[:, n * piece : (n + 1) * piece], gbuf[...].reshape(nz * T, cols), 0, 0
        )
        psend[n] = total.astype(BF16)
    copies = []
    for t in range(1, nx):
        other = place.other_x(t)
        copy = remote(psend.at[other], precv.at[x], ps.at[t - 1], pr.at[t - 1], place.at(x=other))
        copy.start()
        copies.append(copy)
    precv[x] = psend[x]
    for copy in copies:
        copy.wait_recv()
    total = precv[0].astype(F32)
    for n in range(1, nx):
        total = total + precv[n].astype(F32)
    ybuf[y] = total.astype(BF16)
    over = remote(ybuf.at[y], ybuf.at[y], ys, yr, place.partner())
    over.start()
    over.wait_recv()
    mine = pl.ds(pl.multiple_of(z * feats + x * piece, piece), piece)
    out[mine] = (ybuf[0].astype(F32) + ybuf[1].astype(F32)).astype(BF16)
    for t in range(1, nx):
        copy = remote(
            out.at[mine], out.at[mine], as_.at[t - 1], ar.at[t - 1], place.at(x=place.other_x(t))
        )
        copy.start()
        copies.append(copy)
    for copy in copies[nx - 1 :]:
        copy.wait_recv()
    ring_z(
        place,
        lambda slot, start, count: out.at[pl.ds(pl.multiple_of(slot * feats + start, 128), count)],
        feats, zs, zr,
    )
    over.wait_send()
    for copy in copies:
        copy.wait_send()


def vmem(count):
    return [pl.BlockSpec(memory_space=pltpu.VMEM)] * count


def shards(nx, nz, layer_input, q, k, v, beta, lg, do):
    heads = nz
    ranks = []
    for s in range(nx * nz * NY):
        x, z, y = s // (nz * NY), (s // NY) % nz, s % NY
        for h in range(heads):
            ranks.append((s * heads + h, ((x * nz + h) * NY + y) * heads + z))
    moved = lax.ppermute(layer_input, ("seq", "head"), ranks)
    xg = lax.all_gather(moved, "head", axis=0, tiled=True)
    sd = jax.ShapeDtypeStruct
    maps, inverse, uw, back = pl.pallas_call(
        maps_kernel,
        out_shape=(
            sd((2, 3 * HD, HD), F32), sd((2, T, T), F32), sd((2, T, 2 * HD), F32), sd((2, T, HD), F32),
        ),
        in_specs=vmem(6), out_specs=tuple(vmem(4)), name="maps",
    )(q, k, v, do, beta, lg)
    dma = pltpu.SemaphoreType.DMA
    sz = pl.pallas_call(
        lambda *refs: scan_kernel(nx, nz, *refs),
        out_shape=sd((2, 2 * HD, HD), F32),
        in_specs=vmem(1), out_specs=vmem(1)[0],
        scratch_shapes=[
            pltpu.VMEM((2, 3 * HD, HD), F32), pltpu.VMEM((nz, 3 * HD, HD), F32),
            pltpu.VMEM((nx, 3 * HD, HD), F32),
            pltpu.VMEM((nz + 1, HD, 2 * HD), F32), pltpu.VMEM((nz + 1, HD, 2 * HD), F32),
            pltpu.VMEM((nx + 1, HD, HD), F32), pltpu.VMEM((nx + 1, HD, HD), F32),
            pltpu.VMEM((2, 2 * HD, HD), F32),
            dma, dma, dma((2, nz // 2)), dma((2, nz // 2)), dma((nx - 1,)), dma((nx - 1,)), dma, dma,
        ],
        compiler_params=pltpu.CompilerParams(collective_id=0, has_side_effects=True), name="scan",
    )(maps)
    dq, dk, dv, d_beta, d_lg = pl.pallas_call(
        grads_kernel,
        out_shape=(
            sd(q.shape, BF16), sd(q.shape, BF16), sd(q.shape, BF16), sd(beta.shape, F32), sd(beta.shape, F32),
        ),
        in_specs=vmem(10), out_specs=tuple(vmem(5)), name="grads",
    )(q, k, v, do, beta, lg, inverse, uw, back, sz)
    feats, cols = layer_input.shape[1], v.shape[1]
    piece = feats // nx
    dw = pl.pallas_call(
        lambda *refs: weight_kernel(nx, nz, *refs),
        out_shape=sd((feats * nz, cols), BF16),
        in_specs=vmem(2), out_specs=vmem(1)[0],
        scratch_shapes=[
            pltpu.VMEM((nz, T, cols), BF16), pltpu.VMEM((nx, piece, cols), BF16),
            pltpu.VMEM((nx, piece, cols), BF16), pltpu.VMEM((2, piece, cols), BF16),
            dma((2, nz // 2)), dma((2, nz // 2)), dma((nx - 1,)), dma((nx - 1,)), dma, dma,
            dma((nx - 1,)), dma((nx - 1,)), dma((2, nz // 2)), dma((2, nz // 2)),
        ],
        compiler_params=pltpu.CompilerParams(collective_id=1, has_side_effects=True), name="weight",
    )(dv, xg)
    return dq, dk, dv, d_beta, d_lg, dw


def solution(mesh):
    nz = mesh.shape["head"]
    nx = mesh.shape["seq"] // (nz * NY)
    split = P("seq", "head")
    return jax.shard_map(
        lambda *args: shards(nx, nz, *args),
        mesh=mesh, in_specs=(split,) * 7, out_specs=(split,) * 5 + (P(None, "head"),),
        check_vma=False,
    )
```

```python
import jax
import jax.numpy as jnp
from jax import lax
from jax.experimental import pallas as pl
from jax.experimental.pallas import tpu as pltpu
from jax.sharding import PartitionSpec as P

HD = 128
T = 128
F32 = jnp.float32
BF16 = jnp.bfloat16
HIGHEST = lax.Precision.HIGHEST
NY = 2


def dot(a, b, ca=1, cb=0):
    return lax.dot_general(
        a, b, (((ca,), (cb,)), ((), ())), precision=HIGHEST, preferred_element_type=F32
    )


def dot_exact(a, b, ca=1, cb=0):
    return lax.dot_general(a, b, (((ca,), (cb,)), ((), ())), preferred_element_type=F32)


def iotas():
    return (
        lax.broadcasted_iota(jnp.int32, (T, T), 0),
        lax.broadcasted_iota(jnp.int32, (T, T), 1),
    )


def unit_inverse(strict_lower):
    line, col = iotas()
    same = (line >= 64) == (col >= 64)
    diag_part = jnp.where(same, strict_lower, 0.0)
    below = jnp.where(same, 0.0, strict_lower)
    inverse = jnp.where(line == col, 1.0, 0.0) - diag_part
    power = dot(diag_part, diag_part)
    covered = 4
    while covered < 64:
        both = dot(jnp.concatenate([power, inverse], 0), power)
        inverse = inverse + both[T:]
        power = both[:T]
        covered = covered * 2
    inverse = inverse + dot(inverse, power)
    return inverse - dot(dot(inverse, below), inverse)


def as_column(row):
    line, col = iotas()
    return jnp.sum(jnp.where(line == col, row, 0.0), axis=1, keepdims=True)


def as_row(column):
    line, col = iotas()
    return jnp.sum(jnp.where(line == col, column, 0.0), axis=0, keepdims=True)


def gate_parts(lg_row):
    line, col = iotas()
    run_col = jnp.sum(jnp.where(col <= line, lg_row, 0.0), axis=1, keepdims=True)
    run_row = as_row(run_col)
    total = jnp.sum(lg_row, axis=1, keepdims=True)
    causal = line >= col
    decay = jnp.where(causal, jnp.exp(jnp.where(causal, run_col - run_row, 0.0)), 0.0)
    return decay, jnp.exp(run_col), jnp.exp(total - run_col), jnp.exp(total)


def local_maps(q, k, v, do, beta_row, lg_row):
    line, col = iotas()
    beta = as_column(beta_row)
    decay, growth, tail, keep = gate_parts(lg_row)
    keys = k.astype(F32)
    scores = decay * dot_exact(q, k, 1, 1)
    lower = beta * jnp.where(line > col, decay * dot_exact(k, k, 1, 1), 0.0)
    inverse = unit_inverse(lower)
    uw = dot(inverse, jnp.concatenate([beta * v.astype(F32), (beta * growth) * keys], 1))
    back = dot(scores, do.astype(F32), 0, 0)
    bw = dot(tail * keys, uw, 0, 0)
    eye = jnp.where(line == col, 1.0, 0.0)
    a = keep * eye - bw[:, HD:]
    b = bw[:, :HD]
    c = dot(growth * q.astype(F32), do.astype(F32), 0, 0) - dot(uw[:, HD:], back, 0, 0)
    return (a, b, c), (inverse, uw, back)


def local_grads(q, k, v, do, beta_row, lg_row, inverse, uw, back, state, adj):
    line, col = iotas()
    beta = as_column(beta_row)
    decay, growth, tail, keep = gate_parts(lg_row)
    queries, keys, values, grads = (m.astype(F32) for m in (q, k, v, do))
    update = uw[:, :HD] - dot(uw[:, HD:], state)
    d_update = back + dot(tail * keys, adj)
    e = dot(inverse, d_update, 0, 0)
    de = jnp.concatenate([grads, e], 0)
    by_state = dot(de, state, 1, 1)
    by_update = dot(de, update, 1, 1)
    nz = dot(update, adj, 1, 1)
    y = decay * by_update[:T]
    xp = -jnp.where(line > col, decay * by_update[T:], 0.0)
    by_key = dot(jnp.concatenate([xp, y], 0), keys)
    r = by_key[:T] - growth * by_state[T:]
    crossed = dot(
        jnp.concatenate([beta * xp, y], 0), jnp.concatenate([keys, queries], 0), 0, 0
    )
    dq = growth * by_state[:T] + by_key[T:]
    tail_nz = tail * nz
    dk_col = crossed + tail_nz
    dk_row = beta * r
    dv = beta * e
    d_beta = jnp.sum(e * values + keys * r, axis=1, keepdims=True)
    d_run = jnp.sum(queries * dq + keys * (dk_row - dk_col), axis=1, keepdims=True)
    last = jnp.sum(tail_nz * keys, axis=(0, 1), keepdims=True) + keep * jnp.sum(
        adj * state, axis=(0, 1), keepdims=True
    )
    d_lg = jnp.sum(jnp.where(line >= col, d_run, 0.0), axis=0, keepdims=True) + last
    return dq, dk_row + dk_col, dv, as_row(d_beta), d_lg


class Place:
    def __init__(self, nx, nz):
        s = lax.axis_index("seq")
        self.nx, self.nz = nx, nz
        self.x = s // (nz * NY)
        self.z = lax.rem(s // NY, nz)
        self.y = lax.rem(s, NY)
        self.h = lax.axis_index("head")

    def at(self, x=None, z=None, y=None):
        x = self.x if x is None else x
        z = self.z if z is None else z
        y = self.y if y is None else y
        return {"seq": (x * self.nz + z) * NY + y}

    def partner(self):
        return self.at(y=1 - self.y)

    def along_z(self, t):
        return self.at(z=lax.rem(self.z + t, self.nz))

    def other_x(self, t):
        return lax.rem(self.x + t, self.nx)

    def along_head(self, t):
        return {"head": lax.rem(self.h + t, self.nz)}

    def swap_to(self):
        return {**self.at(z=lax.rem(self.h + self.nz - 1, self.nz)), "head": self.z}

    def swap_from(self):
        return {**self.at(z=self.h), "head": lax.rem(self.z + 1, self.nz)}

    def greet(self):
        barrier = pltpu.get_barrier_semaphore()
        peers = [self.partner(), self.swap_to(), self.swap_from()]
        peers += [self.along_z(t) for t in range(1, self.nz)]
        peers += [self.along_head(t) for t in range(1, self.nz)]
        peers += [self.at(x=self.other_x(t)) for t in range(1, self.nx)]
        for peer in peers:
            pl.semaphore_signal(
                barrier, inc=1, device_id=peer, device_id_type=pl.DeviceIdType.MESH
            )
        pl.semaphore_wait(barrier, len(peers))


def remote(src, dst, sems, device):
    return pltpu.make_async_remote_copy(
        src_ref=src, dst_ref=dst, send_sem=sems[0], recv_sem=sems[1],
        device_id=device, device_id_type=pl.DeviceIdType.MESH,
    )


def begin(copies, sent):
    for copy in copies:
        copy.start()
    sent += copies
    return copies


def arrive(copies):
    for copy in copies:
        copy.wait_recv()


def ring_z(place, view, sems, sent):
    nz, z = place.nz, place.z
    steps = nz // 2
    before = [None, None]
    for t in range(1, steps + 1):
        for way, away, ahead in ((0, nz - t + 1, 1), (1, t - 1, nz - 1)):
            src = view(lax.rem(z + away, nz), way if t == steps else None)
            if before[way] is not None:
                before[way].wait_recv()
            copy = remote(src, src, sems(way, t - 1), place.along_z(ahead))
            copy.start()
            sent.append(copy)
            before[way] = copy
        yield t
    arrive(before)


def compose(out, later, earlier):
    a, below = later[0:HD], earlier[0:HD]
    ab = dot(a, jnp.concatenate([below, earlier[HD : 2 * HD]], 1))
    c = earlier[2 * HD : 3 * HD] + dot(below, later[2 * HD : 3 * HD], 0, 0)
    b = ab[:, HD:] + later[HD : 2 * HD]
    out[0:HD] = ab[:, :HD]
    out[HD : 2 * HD] = b
    out[2 * HD : 3 * HD] = c


def chains(blocks, count, forth, aback):
    def step(n, carry):
        m = count - 1 - n
        forth[n + 1] = dot(blocks[n, 0:HD], forth[n]) + blocks[n, HD : 2 * HD]
        aback[m] = dot(blocks[m, 0:HD], aback[m + 1], 0, 0) + blocks[m, 2 * HD : 3 * HD]
        return carry

    lax.fori_loop(0, count, step, 0)


def layer_kernel(
    nx, nz, li, q, k, v, do, beta, lg, dq, dk, dv, d_beta, d_lg, dw,
    theirs, their_gates, xg, inverse, uw, back, pair, zbuf, left, right, joined, xbuf, xf, xb, both,
    ret, ret_gate, got_gate, g, psend, precv, ybuf, *sem_refs
):
    in_s, sw_s, hd_s, z_s, x_s, ret_s, g_s, p_s, y_s, ax_s, az_s = (
        (lambda a, b: lambda *i: (a.at[i], b.at[i]))(sem_refs[2 * n], sem_refs[2 * n + 1])
        for n in range(11)
    )
    place = Place(nx, nz)
    x, z, y, h = place.x, place.z, place.y, place.h
    mine = pl.ds(pl.multiple_of(y * HD, HD), HD)
    yours = pl.ds(pl.multiple_of((1 - y) * HD, HD), HD)
    sent = []
    place.greet()

    asked = [
        remote(ref.at[:, yours], theirs.at[n], in_s(n), place.partner())
        for n, ref in enumerate((q, k, v, do))
    ]
    asked += [
        remote(ref, their_gates.at[n], in_s(4 + n), place.partner())
        for n, ref in enumerate((beta, lg))
    ]
    begin(asked, sent)
    swapped = begin([remote(li, xg.at[z], sw_s(0), place.swap_to())], sent)

    line, col = iotas()
    zero = jnp.zeros((HD, HD), F32)
    for ref in (left, right):
        for n in range(2):
            ref[n, 0:HD] = jnp.where(line == col, 1.0, 0.0)
            ref[n, HD : 2 * HD] = zero
            ref[n, 2 * HD : 3 * HD] = zero
    xf[0] = zero
    xb[nx] = zero
    ret_gate[...] = jnp.zeros_like(ret_gate)

    def inputs(n):
        if n == 0:
            parts = [ref[:, mine] for ref in (q, k, v, do)]
            return parts + [beta[pl.ds(y, 1), :], lg[pl.ds(y, 1), :]]
        parts = [theirs[i] for i in range(4)]
        return parts + [their_gates[i, pl.ds(y, 1), :] for i in range(2)]

    for n in range(2):
        if n == 1:
            arrive(asked)
        (a, b, c), (inv, u, f) = local_maps(*inputs(n))
        slot = y if n == 0 else 1 - y
        pair[slot, 0:HD] = a
        pair[slot, HD : 2 * HD] = b
        pair[slot, 2 * HD : 3 * HD] = c
        inverse[n] = inv
        uw[n] = u
        back[n] = f

    compose(zbuf.at[z], pair.at[1], pair.at[0])
    part_rows = 3 * HD // 2

    def zview(slot, part):
        return zbuf.at[slot] if part is None else zbuf.at[slot, pl.ds(part * part_rows, part_rows)]

    def fold(t):
        wrapped = (z < t).astype(jnp.int32)
        acc = left.at[wrapped]
        compose(acc, acc, zbuf.at[lax.rem(z + nz - t, nz)])
        if t < nz // 2:
            wrapped = (z + t >= nz).astype(jnp.int32)
            acc = right.at[wrapped]
            compose(acc, zbuf.at[lax.rem(z + t, nz)], acc)

    for t in ring_z(place, zview, z_s, sent):
        if t == 1:
            arrive(swapped)
            spread = begin(
                [
                    remote(xg.at[h], xg.at[h], hd_s(n - 1), place.along_head(n))
                    for n in range(1, nz)
                ],
                sent,
            )
        else:
            fold(t - 1)
    fold(nz // 2)
    compose(joined.at[0], left.at[0], right.at[1])
    compose(joined.at[1], left.at[1], right.at[0])
    compose(joined.at[2], zbuf.at[z], joined.at[0])
    compose(xbuf.at[x], joined.at[1], joined.at[2])
    totals = begin(
        [
            remote(xbuf.at[x], xbuf.at[x], x_s(t - 1), place.at(x=place.other_x(t)))
            for t in range(1, nx)
        ],
        sent,
    )
    arrive(totals)
    chains(xbuf, nx, xf, xb)
    state = dot(joined[0, 0:HD], xf[x]) + joined[0, HD : 2 * HD]
    adj = dot(joined[1, 0:HD], xb[x + 1], 0, 0) + joined[1, 2 * HD : 3 * HD]
    both[0, 0:HD] = state
    both[0, HD : 2 * HD] = dot(pair[1, 0:HD], adj, 0, 0) + pair[1, 2 * HD : 3 * HD]
    both[1, 0:HD] = dot(pair[0, 0:HD], state) + pair[0, HD : 2 * HD]
    both[1, HD : 2 * HD] = adj

    def grads(n):
        slot = y if n == 0 else 1 - y
        return local_grads(
            *inputs(n), inverse[n], uw[n], back[n], both[slot, 0:HD], both[slot, HD : 2 * HD]
        )

    gq, gk, gv, gb, gl = grads(1)
    ret[2] = gv.astype(BF16)
    given = begin([remote(ret.at[2], g.at[1, z], ret_s(2), place.partner())], sent)
    ret[0] = gq.astype(BF16)
    ret[1] = gk.astype(BF16)
    ret_gate[0:1] = gb
    ret_gate[1:2] = gl
    returned = begin(
        [
            remote(ret.at[0], dq.at[:, mine], ret_s(0), place.partner()),
            remote(ret.at[1], dk.at[:, mine], ret_s(1), place.partner()),
            remote(ret_gate, got_gate, ret_s(3), place.partner()),
        ],
        sent,
    )
    gq, gk, gv, gb, gl = grads(0)
    g[0, z] = gv.astype(BF16)

    def share(p):
        return begin(
            [
                remote(g.at[p, z], g.at[p, z], g_s(p, t - 1), place.along_z(t))
                for t in range(1, nz)
            ],
            sent,
        )

    shared = [share(0)]
    arrive(given)
    shared.append(share(1))
    dq[:, mine] = gq.astype(BF16)
    dk[:, mine] = gk.astype(BF16)
    dv[:, mine] = gv.astype(BF16)
    dv[:, yours] = g[1, z]
    d_beta[pl.ds(y, 1), :] = gb
    d_lg[pl.ds(y, 1), :] = gl

    arrive(spread)
    feats = xg[...].reshape(nz * T, xg.shape[2])
    scattered = []
    for p in range(2):
        arrive(shared[p])
        total = dot_exact(g[p].reshape(nz * T, HD), feats, 0, 0)
        for n in range(nx):
            psend[p, n] = total[:, n * HD : (n + 1) * HD].astype(BF16)
        scattered.append(
            begin(
                [
                    remote(
                        psend.at[p, place.other_x(t)], precv.at[p, x], p_s(p, t - 1),
                        place.at(x=place.other_x(t)),
                    )
                    for t in range(1, nx)
                ],
                sent,
            )
        )
        precv[p, x] = psend[p, x]
    over = []
    for p in range(2):
        arrive(scattered[p])
        total = precv[p, 0].astype(F32)
        for n in range(1, nx):
            total = total + precv[p, n].astype(F32)
        who = y if p == 0 else 1 - y
        ybuf[who, y] = total.astype(BF16)
        over += begin(
            [remote(ybuf.at[who, y], ybuf.at[who, y], y_s(p), place.partner())], sent
        )

    def chunk(slot):
        return lax.rem(slot + 1, nz)

    arrive(over)
    for p in range(2):
        total = ybuf[p, 0].astype(F32) + ybuf[p, 1].astype(F32)
        dw[p, chunk(z), x] = total.T.astype(BF16)
    one, two = y, 1 - y
    half = nx // 2
    by_x = begin(
        [
            remote(
                dw.at[one, chunk(z), x], dw.at[one, chunk(z), x], ax_s(0, t - 1),
                place.at(x=place.other_x(t)),
            )
            for t in range(1, nx)
        ],
        sent,
    )

    def view_wide(slot, part):
        if part is None:
            return dw.at[one, chunk(slot)]
        return dw.at[one, chunk(slot), pl.ds(part * half, half)]

    def view_narrow(slot, part):
        if part is None:
            return dw.at[two, chunk(slot), x]
        return dw.at[two, chunk(slot), x, pl.ds(part * (HD // 2), HD // 2)]

    narrow = ring_z(place, view_narrow, lambda *i: az_s(1, *i), sent)
    wide = ring_z(place, view_wide, lambda *i: az_s(0, *i), sent)
    next(narrow)
    arrive(by_x)
    next(wide)
    for _ in narrow:
        next(wide)
    by_x = begin(
        [
            remote(dw.at[two, :, x], dw.at[two, :, x], ax_s(1, t - 1), place.at(x=place.other_x(t)))
            for t in range(1, nx)
        ],
        sent,
    )
    for _ in wide:
        pass
    arrive(returned)
    d_beta[pl.ds(1 - y, 1), :] = got_gate[0:1]
    d_lg[pl.ds(1 - y, 1), :] = got_gate[1:2]
    arrive(by_x)
    for copy in sent:
        copy.wait_send()


def finish_kernel(*refs):
    ins, outs = refs[:6], refs[6:]
    for src, dst in zip(ins[:5], outs[:5]):
        dst[...] = src[...]
    heads, nz, nx = ins[5].shape[:3]
    for c in range(nz):
        for n in range(nx):
            for p in range(heads):
                rows = pl.ds((c * nx + n) * HD, HD)
                outs[5][rows, p * HD : (p + 1) * HD] = ins[5][p, c, n]


def vmem(count):
    return [pl.BlockSpec(memory_space=pltpu.VMEM)] * count


def shards(nx, nz, layer_input, q, k, v, beta, lg, do):
    sd = jax.ShapeDtypeStruct
    rows = sd((2, T), F32)
    wide = sd(q.shape, BF16)
    scratch = pltpu.VMEM
    sems = [
        (6,), (1,), (nz - 1,), (2, nz // 2), (nx - 1,), (4,), (2, nz - 1), (2, nx - 1), (2,),
        (2, nx - 1), (2, 2, nz // 2),
    ]
    outs = pl.pallas_call(
        lambda *refs: layer_kernel(nx, nz, *refs),
        out_shape=(wide, wide, wide, rows, rows, sd((2, nz, nx, HD, HD), BF16)),
        in_specs=vmem(7), out_specs=tuple(vmem(6)),
        scratch_shapes=[
            scratch((4, T, HD), BF16), scratch((2, 2, T), F32),
            scratch((nz, T, layer_input.shape[1]), BF16),
            scratch((2, T, T), F32), scratch((2, T, 2 * HD), F32), scratch((2, T, HD), F32),
            scratch((2, 3 * HD, HD), F32), scratch((nz, 3 * HD, HD), F32),
            scratch((2, 3 * HD, HD), F32), scratch((2, 3 * HD, HD), F32), scratch((3, 3 * HD, HD), F32),
            scratch((nx, 3 * HD, HD), F32), scratch((nx + 1, HD, HD), F32), scratch((nx + 1, HD, HD), F32),
            scratch((2, 2 * HD, HD), F32),
            scratch((3, T, HD), BF16), scratch((8, T), F32), scratch((8, T), F32),
            scratch((2, nz, T, HD), BF16), scratch((2, nx, HD, HD), BF16), scratch((2, nx, HD, HD), BF16),
            scratch((2, 2, HD, HD), BF16),
        ]
        + [pltpu.SemaphoreType.DMA(shape) for shape in sems for _ in range(2)],
        compiler_params=pltpu.CompilerParams(
            collective_id=0, has_side_effects=True, vmem_limit_bytes=48 * 2**20
        ),
        name="layer",
    )(layer_input, q, k, v, do, beta.T, lg.T)
    dq, dk, dv, d_beta, d_lg, dw = pl.pallas_call(
        finish_kernel,
        out_shape=(wide, wide, wide, rows, rows, sd((nz * nx * HD, v.shape[1]), BF16)),
        in_specs=vmem(6), out_specs=tuple(vmem(6)), name="finish",
    )(*outs)
    return dq, dk, dv, d_beta.T, d_lg.T, dw


def solution(mesh):
    nz = mesh.shape["head"]
    nx = mesh.shape["seq"] // (nz * NY)
    split = P("seq", "head")
    return jax.shard_map(
        lambda *args: shards(nx, nz, *args),
        mesh=mesh, in_specs=(split,) * 7, out_specs=(split,) * 5 + (P(None, "head"),),
        check_vma=False,
    )
```

```python
import jax
import jax.numpy as jnp
from jax import lax
from jax.experimental import pallas as pl
from jax.experimental.pallas import tpu as pltpu
from jax.sharding import PartitionSpec as P

HD = 128
T = 128
F32 = jnp.float32
BF16 = jnp.bfloat16
HIGHEST = lax.Precision.HIGHEST
NY = 2


def dot(a, b, ca=1, cb=0):
    return lax.dot_general(
        a, b, (((ca,), (cb,)), ((), ())), precision=HIGHEST, preferred_element_type=F32
    )


def dot_exact(a, b, ca=1, cb=0):
    return lax.dot_general(a, b, (((ca,), (cb,)), ((), ())), preferred_element_type=F32)


def iotas():
    return (
        lax.broadcasted_iota(jnp.int32, (T, T), 0),
        lax.broadcasted_iota(jnp.int32, (T, T), 1),
    )


def unit_inverse(strict_lower):
    line, col = iotas()
    same = (line >= 64) == (col >= 64)
    diag_part = jnp.where(same, strict_lower, 0.0)
    below = jnp.where(same, 0.0, strict_lower)
    inverse = jnp.where(line == col, 1.0, 0.0) - diag_part
    power = dot(diag_part, diag_part)
    covered = 4
    while covered < 64:
        both = dot(jnp.concatenate([power, inverse], 0), power)
        inverse = inverse + both[T:]
        power = both[:T]
        covered = covered * 2
    inverse = inverse + dot(inverse, power)
    return inverse - dot(dot(inverse, below), inverse)


def as_column(row):
    line, col = iotas()
    return jnp.sum(jnp.where(line == col, row, 0.0), axis=1, keepdims=True)


def as_row(column):
    line, col = iotas()
    return jnp.sum(jnp.where(line == col, column, 0.0), axis=0, keepdims=True)


def gate_parts(lg_row):
    line, col = iotas()
    run_col = jnp.sum(jnp.where(col <= line, lg_row, 0.0), axis=1, keepdims=True)
    run_row = as_row(run_col)
    total = jnp.sum(lg_row, axis=1, keepdims=True)
    causal = line >= col
    decay = jnp.where(causal, jnp.exp(jnp.where(causal, run_col - run_row, 0.0)), 0.0)
    return decay, jnp.exp(run_col), jnp.exp(total - run_col), jnp.exp(total)


def local_maps(q, k, v, do, beta_row, lg_row):
    line, col = iotas()
    beta = as_column(beta_row)
    decay, growth, tail, keep = gate_parts(lg_row)
    keys = k.astype(F32)
    scores = decay * dot_exact(q, k, 1, 1)
    lower = beta * jnp.where(line > col, decay * dot_exact(k, k, 1, 1), 0.0)
    inverse = unit_inverse(lower)
    uw = dot(inverse, jnp.concatenate([beta * v.astype(F32), (beta * growth) * keys], 1))
    back = dot(scores, do.astype(F32), 0, 0)
    bw = dot(tail * keys, uw, 0, 0)
    eye = jnp.where(line == col, 1.0, 0.0)
    a = keep * eye - bw[:, HD:]
    b = bw[:, :HD]
    c = dot(growth * q.astype(F32), do.astype(F32), 0, 0) - dot(uw[:, HD:], back, 0, 0)
    return (a, b, c), (inverse, uw, back)


def local_grads(q, k, v, do, beta_row, lg_row, inverse, uw, back, state, adj):
    line, col = iotas()
    beta = as_column(beta_row)
    decay, growth, tail, keep = gate_parts(lg_row)
    queries, keys, values, grads = (m.astype(F32) for m in (q, k, v, do))
    update = uw[:, :HD] - dot(uw[:, HD:], state)
    d_update = back + dot(tail * keys, adj)
    e = dot(inverse, d_update, 0, 0)
    de = jnp.concatenate([grads, e], 0)
    by_state = dot(de, state, 1, 1)
    by_update = dot(de, update, 1, 1)
    nz = dot(update, adj, 1, 1)
    y = decay * by_update[:T]
    xp = -jnp.where(line > col, decay * by_update[T:], 0.0)
    by_key = dot(jnp.concatenate([xp, y], 0), keys)
    r = by_key[:T] - growth * by_state[T:]
    crossed = dot(
        jnp.concatenate([beta * xp, y], 0), jnp.concatenate([keys, queries], 0), 0, 0
    )
    dq = growth * by_state[:T] + by_key[T:]
    tail_nz = tail * nz
    dk_col = crossed + tail_nz
    dk_row = beta * r
    dv = beta * e
    d_beta = jnp.sum(e * values + keys * r, axis=1, keepdims=True)
    d_run = jnp.sum(queries * dq + keys * (dk_row - dk_col), axis=1, keepdims=True)
    last = jnp.sum(tail_nz * keys, axis=(0, 1), keepdims=True) + keep * jnp.sum(
        adj * state, axis=(0, 1), keepdims=True
    )
    d_lg = jnp.sum(jnp.where(line >= col, d_run, 0.0), axis=0, keepdims=True) + last
    return dq, dk_row + dk_col, dv, as_row(d_beta), d_lg


class Place:
    def __init__(self, nx, nz):
        s = lax.axis_index("seq")
        self.nx, self.nz = nx, nz
        self.x = s // (nz * NY)
        self.z = lax.rem(s // NY, nz)
        self.y = lax.rem(s, NY)
        self.h = lax.axis_index("head")

    def at(self, x=None, z=None, y=None):
        x = self.x if x is None else x
        z = self.z if z is None else z
        y = self.y if y is None else y
        return {"seq": (x * self.nz + z) * NY + y}

    def partner(self):
        return self.at(y=1 - self.y)

    def along_z(self, t):
        return self.at(z=lax.rem(self.z + t, self.nz))

    def other_x(self, t):
        return lax.rem(self.x + t, self.nx)

    def along_head(self, t):
        return {"head": lax.rem(self.h + t, self.nz)}

    def swap_to(self):
        return {**self.at(z=lax.rem(self.h + self.nz - 1, self.nz)), "head": self.z}

    def swap_from(self):
        return {**self.at(z=self.h), "head": lax.rem(self.z + 1, self.nz)}

    def greet(self):
        barrier = pltpu.get_barrier_semaphore()
        peers = [self.partner(), self.swap_to(), self.swap_from()]
        peers += [self.along_z(t) for t in range(1, self.nz)]
        peers += [self.along_head(t) for t in range(1, self.nz)]
        peers += [self.at(x=self.other_x(t)) for t in range(1, self.nx)]
        for peer in peers:
            pl.semaphore_signal(
                barrier, inc=1, device_id=peer, device_id_type=pl.DeviceIdType.MESH
            )
        pl.semaphore_wait(barrier, len(peers))


def remote(src, dst, sems, device):
    return pltpu.make_async_remote_copy(
        src_ref=src, dst_ref=dst, send_sem=sems[0], recv_sem=sems[1],
        device_id=device, device_id_type=pl.DeviceIdType.MESH,
    )


def begin(copies, sent):
    for copy in copies:
        copy.start()
    sent += copies
    return copies


def arrive(copies):
    for copy in copies:
        copy.wait_recv()


def ring_z(place, view, sems, sent):
    nz, z = place.nz, place.z
    steps = nz // 2
    before = {}
    for t in range(1, steps + 1):
        for part in range(2):
            for way, away, ahead in ((0, nz - t + 1, 1), (1, t - 1, nz - 1)):
                if (way, part) in before:
                    before.pop((way, part)).wait_recv()
                if t == steps and part != way:
                    continue
                src = view(lax.rem(z + away, nz), part)
                copy = remote(src, src, sems(way, part, t - 1), place.along_z(ahead))
                copy.start()
                sent.append(copy)
                before[way, part] = copy
        yield t
    arrive(before.values())


OFFSET, MAP, ADJ = slice(0, HD), slice(HD, 2 * HD), slice(2 * HD, 3 * HD)


def compose(out, later, earlier):
    a, below = later[MAP], earlier[MAP]
    ab = dot(a, jnp.concatenate([below, earlier[OFFSET]], 1))
    c = earlier[ADJ] + dot(below, later[ADJ], 0, 0)
    b = ab[:, HD:] + later[OFFSET]
    out[MAP] = ab[:, :HD]
    out[OFFSET] = b
    out[ADJ] = c


def chains(blocks, count, forth, aback):
    def step(n, carry):
        m = count - 1 - n
        forth[n + 1] = dot(blocks[n, MAP], forth[n]) + blocks[n, OFFSET]
        aback[m] = dot(blocks[m, MAP], aback[m + 1], 0, 0) + blocks[m, ADJ]
        return carry

    lax.fori_loop(0, count, step, 0)


def layer_kernel(
    nx, nz, li, q, k, v, do, beta, lg, dq, dk, dv, d_beta, d_lg, dw,
    inp, gates, xg, inverse, uw, back, pair, zbuf, left, right, joined, xbuf, xf, xb, both,
    ret, ret_gate, got_gate, g, psend, precv, ybuf, load_sems, *sem_refs
):
    in_s, sw_s, hd_s, z_s, x_s, ret_s, g_s, p_s, y_s, ax_s, an_s, az_s = (
        (lambda a, b: lambda *i: (a.at[i], b.at[i]))(sem_refs[2 * n], sem_refs[2 * n + 1])
        for n in range(12)
    )
    place = Place(nx, nz)
    x, z, y, h = place.x, place.z, place.y, place.h
    mine = pl.ds(pl.multiple_of(y * HD, HD), HD)
    yours = pl.ds(pl.multiple_of((1 - y) * HD, HD), HD)
    sent = []
    loads = [
        pltpu.make_async_copy(ref.at[:, mine], inp.at[0, n], load_sems.at[n])
        for n, ref in enumerate((q, k, v, do))
    ]
    loads += [
        pltpu.make_async_copy(ref, gates.at[0, n], load_sems.at[4 + n])
        for n, ref in enumerate((beta, lg))
    ]
    for load in loads:
        load.start()
    place.greet()

    asked = [
        remote(ref.at[:, yours], inp.at[1, n], in_s(n), place.partner())
        for n, ref in enumerate((q, k, v, do))
    ]
    asked += [
        remote(ref, gates.at[1, n], in_s(4 + n), place.partner())
        for n, ref in enumerate((beta, lg))
    ]
    begin(asked, sent)
    swapped = begin([remote(li, xg.at[z], sw_s(0), place.swap_to())], sent)

    line, col = iotas()
    zero = jnp.zeros((HD, HD), F32)
    for ref in (left, right):
        for n in range(2):
            ref[n, MAP] = jnp.where(line == col, 1.0, 0.0)
            ref[n, OFFSET] = zero
            ref[n, ADJ] = zero
    xf[0] = zero
    xb[nx] = zero
    ret_gate[...] = jnp.zeros_like(ret_gate)
    for load in loads:
        load.wait()

    def inputs(n):
        return [inp[n, i] for i in range(4)] + [gates[n, i, pl.ds(y, 1), :] for i in range(2)]

    def maps_of(n, carry):
        @pl.when(n == 1)
        def _():
            arrive(asked)

        (a, b, c), (inv, u, f) = local_maps(*inputs(n))
        slot = lax.rem(y + n, 2)
        pair[slot, MAP] = a
        pair[slot, OFFSET] = b
        pair[slot, ADJ] = c
        inverse[n] = inv
        uw[n] = u
        back[n] = f
        return carry

    lax.fori_loop(0, 2, maps_of, 0)
    compose(zbuf.at[z], pair.at[1], pair.at[0])
    part_rows = 3 * HD // 2

    def zview(slot, part):
        return zbuf.at[slot, pl.ds(part * part_rows, part_rows)]

    def fold(t):
        wrapped = (z < t).astype(jnp.int32)
        acc = left.at[wrapped]
        compose(acc, acc, zbuf.at[lax.rem(z + nz - t, nz)])
        if t < nz // 2:
            wrapped = (z + t >= nz).astype(jnp.int32)
            acc = right.at[wrapped]
            compose(acc, zbuf.at[lax.rem(z + t, nz)], acc)

    for t in ring_z(place, zview, z_s, sent):
        if t == 1:
            arrive(swapped)
            spread = begin(
                [
                    remote(xg.at[h], xg.at[h], hd_s(n - 1), place.along_head(n))
                    for n in range(1, nz)
                ],
                sent,
            )
        else:
            fold(t - 1)
    fold(nz // 2)
    compose(joined.at[0], left.at[0], right.at[1])
    compose(joined.at[1], left.at[1], right.at[0])
    compose(joined.at[2], zbuf.at[z], joined.at[0])
    compose(xbuf.at[x], joined.at[1], joined.at[2])
    totals = []
    for t in range(1, nx):
        other = place.other_x(t)
        low = jnp.where(other > x, 0, HD)
        rows = xbuf.at[x, pl.ds(pl.multiple_of(low, HD), 2 * HD)]
        totals.append(remote(rows, rows, x_s(t - 1), place.at(x=other)))
    begin(totals, sent)
    arrive(totals)
    chains(xbuf, nx, xf, xb)
    state = dot(joined[0, MAP], xf[x]) + joined[0, OFFSET]
    adj = dot(joined[1, MAP], xb[x + 1], 0, 0) + joined[1, ADJ]
    both[0, 0] = state
    both[0, 1] = dot(pair[1, MAP], adj, 0, 0) + pair[1, ADJ]
    both[1, 0] = dot(pair[0, MAP], state) + pair[0, OFFSET]
    both[1, 1] = adj

    given = [remote(ret.at[1, 2], g.at[1, z], ret_s(2), place.partner())]
    returned = [
        remote(ret.at[1, 0], dq.at[:, mine], ret_s(0), place.partner()),
        remote(ret.at[1, 1], dk.at[:, mine], ret_s(1), place.partner()),
        remote(ret_gate.at[1], got_gate, ret_s(3), place.partner()),
    ]

    def grads_of(turn, carry):
        n = 1 - turn
        slot = lax.rem(y + n, 2)
        gq, gk, gv, gb, gl = local_grads(
            *inputs(n), inverse[n], uw[n], back[n], both[slot, 0], both[slot, 1]
        )
        ret[n, 0] = gq.astype(BF16)
        ret[n, 1] = gk.astype(BF16)
        ret[n, 2] = gv.astype(BF16)
        ret_gate[n, 0:1] = gb
        ret_gate[n, 1:2] = gl

        @pl.when(turn == 0)
        def _():
            for copy in given + returned:
                copy.start()

        return carry

    lax.fori_loop(0, 2, grads_of, 0)
    sent += given + returned
    g[0, z] = ret[0, 2]

    def share(p):
        return begin(
            [
                remote(g.at[p, z], g.at[p, z], g_s(p, t - 1), place.along_z(t))
                for t in range(1, nz)
            ],
            sent,
        )

    shared = [share(0)]
    arrive(given)
    shared.append(share(1))
    dq[:, mine] = ret[0, 0]
    dk[:, mine] = ret[0, 1]
    dv[:, mine] = ret[0, 2]
    dv[:, yours] = g[1, z]
    d_beta[pl.ds(y, 1), :] = ret_gate[0, 0:1]
    d_lg[pl.ds(y, 1), :] = ret_gate[0, 1:2]

    arrive(spread)
    scattered = []
    for p in range(2):
        arrive(shared[p])
        feats = xg[...].reshape(nz * T, xg.shape[2])
        total = dot_exact(g[p].reshape(nz * T, HD), feats, 0, 0)
        for n in range(nx):
            psend[p, n] = total[:, n * HD : (n + 1) * HD].astype(BF16)
        scattered.append(
            begin(
                [
                    remote(
                        psend.at[p, place.other_x(t)], precv.at[p, x], p_s(p, t - 1),
                        place.at(x=place.other_x(t)),
                    )
                    for t in range(1, nx)
                ],
                sent,
            )
        )
        precv[p, x] = psend[p, x]
    over = []
    for p in range(2):
        arrive(scattered[p])
        total = precv[p, 0].astype(F32)
        for n in range(1, nx):
            total = total + precv[p, n].astype(F32)
        who = y if p == 0 else 1 - y
        ybuf[who, y] = total.astype(BF16)
        over += begin(
            [remote(ybuf.at[who, y], ybuf.at[who, y], y_s(p), place.partner())], sent
        )

    def chunk(slot):
        return lax.rem(slot + 1, nz)

    arrive(over)
    for p in range(2):
        total = ybuf[p, 0].astype(F32) + ybuf[p, 1].astype(F32)
        dw[p, chunk(z), x] = total.T.astype(BF16)

    one, two = y, 1 - y
    piece = dw.at[one, chunk(z), x]
    by_x = begin(
        [remote(piece, piece, ax_s(0, t - 1), place.at(x=place.other_x(t))) for t in range(1, nx)],
        sent,
    )
    piece = dw.at[two, chunk(z), x]
    by_z = begin(
        [remote(piece, piece, an_s(t - 1), place.along_z(t)) for t in range(1, nz)], sent
    )
    half = nx // 2
    wide = ring_z(
        place, lambda slot, part: dw.at[one, chunk(slot), pl.ds(part * half, half)], az_s, sent
    )
    arrive(by_x)
    next(wide)
    arrive(by_z)
    pieces = dw.at[two, :, x]
    by_x = begin(
        [remote(pieces, pieces, ax_s(1, t - 1), place.at(x=place.other_x(t))) for t in range(1, nx)],
        sent,
    )
    for _ in wide:
        pass
    arrive(returned)
    d_beta[pl.ds(1 - y, 1), :] = got_gate[0:1]
    d_lg[pl.ds(1 - y, 1), :] = got_gate[1:2]
    arrive(by_x)
    for copy in sent:
        copy.wait_send()


def finish_kernel(*refs):
    ins, outs = refs[:6], refs[6:]
    for src, dst in zip(ins[:5], outs[:5]):
        dst[...] = src[...]
    heads, nz, nx = ins[5].shape[:3]
    for c in range(nz):
        for n in range(nx):
            for p in range(heads):
                rows = pl.ds((c * nx + n) * HD, HD)
                outs[5][rows, p * HD : (p + 1) * HD] = ins[5][p, c, n]


def vmem(count):
    return [pl.BlockSpec(memory_space=pltpu.VMEM)] * count


def shards(nx, nz, layer_input, q, k, v, beta, lg, do):
    sd = jax.ShapeDtypeStruct
    rows = sd((2, T), F32)
    wide = sd(q.shape, BF16)
    scratch = pltpu.VMEM
    sems = [
        (6,), (1,), (nz - 1,), (2, 2, nz // 2), (nx - 1,), (4,), (2, nz - 1), (2, nx - 1), (2,),
        (2, nx - 1), (nz - 1,), (2, 2, nz // 2),
    ]
    outs = pl.pallas_call(
        lambda *refs: layer_kernel(nx, nz, *refs),
        out_shape=(wide, wide, wide, rows, rows, sd((2, nz, nx, HD, HD), BF16)),
        in_specs=[pl.BlockSpec(memory_space=pltpu.HBM)] * 7, out_specs=tuple(vmem(6)),
        scratch_shapes=[
            scratch((2, 4, T, HD), BF16), scratch((2, 2, 2, T), F32),
            scratch((nz, T, layer_input.shape[1]), BF16),
            scratch((2, T, T), F32), scratch((2, T, 2 * HD), F32), scratch((2, T, HD), F32),
            scratch((2, 3 * HD, HD), F32), scratch((nz, 3 * HD, HD), F32),
            scratch((2, 3 * HD, HD), F32), scratch((2, 3 * HD, HD), F32), scratch((3, 3 * HD, HD), F32),
            scratch((nx, 3 * HD, HD), F32), scratch((nx + 1, HD, HD), F32), scratch((nx + 1, HD, HD), F32),
            scratch((2, 2, HD, HD), F32),
            scratch((2, 3, T, HD), BF16), scratch((2, 8, T), F32), scratch((8, T), F32),
            scratch((2, nz, T, HD), BF16), scratch((2, nx, HD, HD), BF16), scratch((2, nx, HD, HD), BF16),
            scratch((2, 2, HD, HD), BF16), pltpu.SemaphoreType.DMA((6,)),
        ]
        + [pltpu.SemaphoreType.DMA(shape) for shape in sems for _ in range(2)],
        compiler_params=pltpu.CompilerParams(
            collective_id=0, has_side_effects=True, vmem_limit_bytes=62 * 2**20
        ),
        name="layer",
    )(layer_input, q, k, v, do, beta.T, lg.T)
    dq, dk, dv, d_beta, d_lg, dw = pl.pallas_call(
        finish_kernel,
        out_shape=(wide, wide, wide, rows, rows, sd((nz * nx * HD, v.shape[1]), BF16)),
        in_specs=vmem(6), out_specs=tuple(vmem(6)), name="finish",
    )(*outs)
    return dq, dk, dv, d_beta.T, d_lg.T, dw


def solution(mesh):
    nz = mesh.shape["head"]
    nx = mesh.shape["seq"] // (nz * NY)
    split = P("seq", "head")
    return jax.shard_map(
        lambda *args: shards(nx, nz, *args),
        mesh=mesh, in_specs=(split,) * 7, out_specs=(split,) * 5 + (P(None, "head"),),
        check_vma=False,
    )
```

```python
import jax
import jax.numpy as jnp
from jax import lax
from jax.experimental import pallas as pl
from jax.experimental.pallas import tpu as pltpu
from jax.sharding import PartitionSpec as P

HD = 128
T = 128
F32 = jnp.float32
BF16 = jnp.bfloat16
HIGHEST = lax.Precision.HIGHEST
NY = 2


def dot(a, b, ca=1, cb=0):
    return lax.dot_general(
        a, b, (((ca,), (cb,)), ((), ())), precision=HIGHEST, preferred_element_type=F32
    )


def dot_exact(a, b, ca=1, cb=0):
    return lax.dot_general(a, b, (((ca,), (cb,)), ((), ())), preferred_element_type=F32)


def iotas():
    return (
        lax.broadcasted_iota(jnp.int32, (T, T), 0),
        lax.broadcasted_iota(jnp.int32, (T, T), 1),
    )


def unit_inverse(strict_lower):
    line, col = iotas()
    same = (line >= 64) == (col >= 64)
    diag_part = jnp.where(same, strict_lower, 0.0)
    below = jnp.where(same, 0.0, strict_lower)
    inverse = jnp.where(line == col, 1.0, 0.0) - diag_part
    power = dot(diag_part, diag_part)
    covered = 4
    while covered < 64:
        both = dot(jnp.concatenate([power, inverse], 0), power)
        inverse = inverse + both[T:]
        power = both[:T]
        covered = covered * 2
    inverse = inverse + dot(inverse, power)
    return inverse - dot(dot(inverse, below), inverse)


def as_column(row):
    line, col = iotas()
    return jnp.sum(jnp.where(line == col, row, 0.0), axis=1, keepdims=True)


def as_row(column):
    line, col = iotas()
    return jnp.sum(jnp.where(line == col, column, 0.0), axis=0, keepdims=True)


def gate_parts(lg_row):
    line, col = iotas()
    run_col = jnp.sum(jnp.where(col <= line, lg_row, 0.0), axis=1, keepdims=True)
    run_row = as_row(run_col)
    total = jnp.sum(lg_row, axis=1, keepdims=True)
    causal = line >= col
    decay = jnp.where(causal, jnp.exp(jnp.where(causal, run_col - run_row, 0.0)), 0.0)
    return decay, jnp.exp(run_col), jnp.exp(total - run_col), jnp.exp(total)


def local_maps(q, k, v, do, beta_row, lg_row):
    line, col = iotas()
    beta = as_column(beta_row)
    decay, growth, tail, keep = gate_parts(lg_row)
    keys = k.astype(F32)
    scores = decay * dot_exact(q, k, 1, 1)
    lower = beta * jnp.where(line > col, decay * dot_exact(k, k, 1, 1), 0.0)
    inverse = unit_inverse(lower)
    uw = dot(inverse, jnp.concatenate([beta * v.astype(F32), (beta * growth) * keys], 1))
    back = dot(scores, do.astype(F32), 0, 0)
    bw = dot(tail * keys, uw, 0, 0)
    eye = jnp.where(line == col, 1.0, 0.0)
    a = keep * eye - bw[:, HD:]
    b = bw[:, :HD]
    c = dot(growth * q.astype(F32), do.astype(F32), 0, 0) - dot(uw[:, HD:], back, 0, 0)
    return (a, b, c), (inverse, uw, back)


def local_update(k, beta_row, lg_row, inverse, uw, back, state, adj):
    tail = gate_parts(lg_row)[2]
    update = uw[:, :HD] - dot(uw[:, HD:], state)
    e = dot(inverse, back + dot(tail * k.astype(F32), adj), 0, 0)
    return update, e, as_column(beta_row) * e


def local_grads(q, k, v, do, beta_row, lg_row, update, e, state, adj):
    line, col = iotas()
    beta = as_column(beta_row)
    decay, growth, tail, keep = gate_parts(lg_row)
    queries, keys, values, grads = (m.astype(F32) for m in (q, k, v, do))
    de = jnp.concatenate([grads, e], 0)
    by_state = dot(de, state, 1, 1)
    by_update = dot(de, update, 1, 1)
    nz = dot(update, adj, 1, 1)
    y = decay * by_update[:T]
    xp = -jnp.where(line > col, decay * by_update[T:], 0.0)
    by_key = dot(jnp.concatenate([xp, y], 0), keys)
    r = by_key[:T] - growth * by_state[T:]
    crossed = dot(
        jnp.concatenate([beta * xp, y], 0), jnp.concatenate([keys, queries], 0), 0, 0
    )
    dq = growth * by_state[:T] + by_key[T:]
    tail_nz = tail * nz
    dk_col = crossed + tail_nz
    dk_row = beta * r
    d_beta = jnp.sum(e * values + keys * r, axis=1, keepdims=True)
    d_run = jnp.sum(queries * dq + keys * (dk_row - dk_col), axis=1, keepdims=True)
    last = jnp.sum(tail_nz * keys, axis=(0, 1), keepdims=True) + keep * jnp.sum(
        adj * state, axis=(0, 1), keepdims=True
    )
    d_lg = jnp.sum(jnp.where(line >= col, d_run, 0.0), axis=0, keepdims=True) + last
    return dq, dk_row + dk_col, as_row(d_beta), d_lg


class Place:
    def __init__(self, nx, nz):
        s = lax.axis_index("seq")
        self.nx, self.nz = nx, nz
        self.x = s // (nz * NY)
        self.z = lax.rem(s // NY, nz)
        self.y = lax.rem(s, NY)
        self.h = lax.axis_index("head")

    def at(self, x=None, z=None, y=None):
        x = self.x if x is None else x
        z = self.z if z is None else z
        y = self.y if y is None else y
        return {"seq": (x * self.nz + z) * NY + y}

    def partner(self):
        return self.at(y=1 - self.y)

    def along_z(self, t):
        return self.at(z=lax.rem(self.z + t, self.nz))

    def other_x(self, t):
        return lax.rem(self.x + t, self.nx)

    def along_head(self, t):
        return {"head": lax.rem(self.h + t, self.nz)}

    def swap_to(self):
        return {**self.at(z=lax.rem(self.h + self.nz - 1, self.nz)), "head": self.z}

    def swap_from(self):
        return {**self.at(z=self.h), "head": lax.rem(self.z + 1, self.nz)}

    def greet(self):
        barrier = pltpu.get_barrier_semaphore()
        peers = [self.partner(), self.swap_to(), self.swap_from()]
        peers += [self.along_z(t) for t in range(1, self.nz)]
        peers += [self.along_head(t) for t in range(1, self.nz)]
        peers += [self.at(x=self.other_x(t)) for t in range(1, self.nx)]
        for peer in peers:
            pl.semaphore_signal(
                barrier, inc=1, device_id=peer, device_id_type=pl.DeviceIdType.MESH
            )
        pl.semaphore_wait(barrier, len(peers))


def remote(src, dst, sems, device):
    return pltpu.make_async_remote_copy(
        src_ref=src, dst_ref=dst, send_sem=sems[0], recv_sem=sems[1],
        device_id=device, device_id_type=pl.DeviceIdType.MESH,
    )


def begin(copies, sent):
    for copy in copies:
        copy.start()
    sent += copies
    return copies


def arrive(copies):
    for copy in copies:
        copy.wait_recv()


def ring_z(place, view, sems, sent):
    nz, z = place.nz, place.z
    steps = nz // 2
    before = {}
    for t in range(1, steps + 1):
        for part in range(2):
            for way, away, ahead in ((0, nz - t + 1, 1), (1, t - 1, nz - 1)):
                if (way, part) in before:
                    before.pop((way, part)).wait_recv()
                if t == steps and part != way:
                    continue
                src = view(lax.rem(z + away, nz), part)
                copy = remote(src, src, sems(way, part, t - 1), place.along_z(ahead))
                copy.start()
                sent.append(copy)
                before[way, part] = copy
        yield t
    arrive(before.values())


OFFSET, MAP, ADJ = slice(0, HD), slice(HD, 2 * HD), slice(2 * HD, 3 * HD)


def compose(out, later, earlier):
    a, below = later[MAP], earlier[MAP]
    ab = dot(a, jnp.concatenate([below, earlier[OFFSET]], 1))
    c = earlier[ADJ] + dot(below, later[ADJ], 0, 0)
    b = ab[:, HD:] + later[OFFSET]
    out[MAP] = ab[:, :HD]
    out[OFFSET] = b
    out[ADJ] = c


def chains(blocks, count, forth, aback):
    def step(n, carry):
        m = count - 1 - n
        forth[n + 1] = dot(blocks[n, MAP], forth[n]) + blocks[n, OFFSET]
        aback[m] = dot(blocks[m, MAP], aback[m + 1], 0, 0) + blocks[m, ADJ]
        return carry

    lax.fori_loop(0, count, step, 0)


def layer_kernel(
    nx, nz, li, q, k, v, do, beta, lg, dq, dk, dv, d_beta, d_lg, dw,
    inp, gates, xg, inverse, uw, back, pair, zbuf, left, right, joined, xbuf, xf, xb, both,
    written, ret, ret_gate, got_gate, g, psend, precv, ybuf, load_sems, *sem_refs
):
    in_s, sw_s, hd_s, z_s, x_s, ret_s, g_s, p_s, y_s, ax_s, an_s, az_s, aw_s = (
        (lambda a, b: lambda *i: (a.at[i], b.at[i]))(sem_refs[2 * n], sem_refs[2 * n + 1])
        for n in range(13)
    )
    place = Place(nx, nz)
    x, z, y, h = place.x, place.z, place.y, place.h
    mine = pl.ds(pl.multiple_of(y * HD, HD), HD)
    yours = pl.ds(pl.multiple_of((1 - y) * HD, HD), HD)
    sent = []
    loads = [
        pltpu.make_async_copy(ref.at[:, mine], inp.at[0, n], load_sems.at[n])
        for n, ref in enumerate((q, k, v, do))
    ]
    loads += [
        pltpu.make_async_copy(ref, gates.at[0, n], load_sems.at[4 + n])
        for n, ref in enumerate((beta, lg))
    ]
    for load in loads:
        load.start()
    place.greet()

    asked = [
        remote(ref.at[:, yours], inp.at[1, n], in_s(n), place.partner())
        for n, ref in enumerate((q, k, v, do))
    ]
    asked += [
        remote(ref, gates.at[1, n], in_s(4 + n), place.partner())
        for n, ref in enumerate((beta, lg))
    ]
    begin(asked, sent)
    swapped = begin([remote(li, xg.at[z], sw_s(0), place.swap_to())], sent)

    line, col = iotas()
    zero = jnp.zeros((HD, HD), F32)
    for ref in (left, right):
        for n in range(2):
            ref[n, MAP] = jnp.where(line == col, 1.0, 0.0)
            ref[n, OFFSET] = zero
            ref[n, ADJ] = zero
    xf[0] = zero
    xb[nx] = zero
    ret_gate[...] = jnp.zeros_like(ret_gate)
    for load in loads:
        load.wait()

    def inputs(n):
        return [inp[n, i] for i in range(4)] + [gates[n, i, pl.ds(y, 1), :] for i in range(2)]

    def maps_of(n, carry):
        @pl.when(n == 1)
        def _():
            arrive(asked)

        (a, b, c), (inv, u, f) = local_maps(*inputs(n))
        slot = lax.rem(y + n, 2)
        pair[slot, MAP] = a
        pair[slot, OFFSET] = b
        pair[slot, ADJ] = c
        inverse[n] = inv
        uw[n] = u
        back[n] = f
        return carry

    lax.fori_loop(0, 2, maps_of, 0)
    compose(zbuf.at[z], pair.at[1], pair.at[0])
    part_rows = 3 * HD // 2

    def zview(slot, part):
        return zbuf.at[slot, pl.ds(part * part_rows, part_rows)]

    def fold(t):
        wrapped = (z < t).astype(jnp.int32)
        acc = left.at[wrapped]
        compose(acc, acc, zbuf.at[lax.rem(z + nz - t, nz)])
        if t < nz // 2:
            wrapped = (z + t >= nz).astype(jnp.int32)
            acc = right.at[wrapped]
            compose(acc, zbuf.at[lax.rem(z + t, nz)], acc)

    for t in ring_z(place, zview, z_s, sent):
        if t == 1:
            arrive(swapped)
            spread = begin(
                [
                    remote(xg.at[h], xg.at[h], hd_s(n - 1), place.along_head(n))
                    for n in range(1, nz)
                ],
                sent,
            )
        else:
            fold(t - 1)
    fold(nz // 2)
    compose(joined.at[0], left.at[0], right.at[1])
    compose(joined.at[1], left.at[1], right.at[0])
    compose(joined.at[2], zbuf.at[z], joined.at[0])
    compose(xbuf.at[x], joined.at[1], joined.at[2])
    totals = []
    for t in range(1, nx):
        other = place.other_x(t)
        low = jnp.where(other > x, 0, HD)
        rows = xbuf.at[x, pl.ds(pl.multiple_of(low, HD), 2 * HD)]
        totals.append(remote(rows, rows, x_s(t - 1), place.at(x=other)))
    begin(totals, sent)
    arrive(totals)
    chains(xbuf, nx, xf, xb)
    state = dot(joined[0, MAP], xf[x]) + joined[0, OFFSET]
    adj = dot(joined[1, MAP], xb[x + 1], 0, 0) + joined[1, ADJ]
    both[0, 0] = state
    both[0, 1] = dot(pair[1, MAP], adj, 0, 0) + pair[1, ADJ]
    both[1, 0] = dot(pair[0, MAP], state) + pair[0, OFFSET]
    both[1, 1] = adj

    given = [remote(ret.at[1, 2], g.at[1, z], ret_s(2), place.partner())]
    returned = [
        remote(ret.at[1, 0], dq.at[:, mine], ret_s(0), place.partner()),
        remote(ret.at[1, 1], dk.at[:, mine], ret_s(1), place.partner()),
        remote(ret_gate.at[1], got_gate, ret_s(3), place.partner()),
    ]

    def update_of(turn, carry):
        n = 1 - turn
        slot = lax.rem(y + n, 2)
        parts = inputs(n)
        update, e, gv = local_update(
            parts[1], parts[4], parts[5], inverse[n], uw[n], back[n], both[slot, 0], both[slot, 1]
        )
        written[n, 0] = update
        written[n, 1] = e
        ret[n, 2] = gv.astype(BF16)

        @pl.when(turn == 0)
        def _():
            for copy in given:
                copy.start()

        return carry

    def grads_of(turn, carry):
        n = 1 - turn
        slot = lax.rem(y + n, 2)
        gq, gk, gb, gl = local_grads(
            *inputs(n), written[n, 0], written[n, 1], both[slot, 0], both[slot, 1]
        )
        ret[n, 0] = gq.astype(BF16)
        ret[n, 1] = gk.astype(BF16)
        ret_gate[n, 0:1] = gb
        ret_gate[n, 1:2] = gl

        @pl.when(turn == 0)
        def _():
            for copy in returned:
                copy.start()

        return carry

    def share(p):
        return begin(
            [
                remote(g.at[p, z], g.at[p, z], g_s(p, t - 1), place.along_z(t))
                for t in range(1, nz)
            ],
            sent,
        )

    lax.fori_loop(0, 2, update_of, 0)
    g[0, z] = ret[0, 2]
    shared = [share(0)]
    lax.fori_loop(0, 2, grads_of, 0)
    sent += given + returned
    arrive(given)
    shared.append(share(1))
    dq[:, mine] = ret[0, 0]
    dk[:, mine] = ret[0, 1]
    dv[:, mine] = ret[0, 2]
    dv[:, yours] = g[1, z]
    d_beta[pl.ds(y, 1), :] = ret_gate[0, 0:1]
    d_lg[pl.ds(y, 1), :] = ret_gate[0, 1:2]

    arrive(spread)
    scattered = []
    for p in range(2):
        arrive(shared[p])
        feats = xg[...].reshape(nz * T, xg.shape[2])
        total = dot_exact(g[p].reshape(nz * T, HD), feats, 0, 0)
        for n in range(nx):
            psend[p, n] = total[:, n * HD : (n + 1) * HD].astype(BF16)
        scattered.append(
            begin(
                [
                    remote(
                        psend.at[p, place.other_x(t)], precv.at[p, x], p_s(p, t - 1),
                        place.at(x=place.other_x(t)),
                    )
                    for t in range(1, nx)
                ],
                sent,
            )
        )
        precv[p, x] = psend[p, x]
    over = []
    for p in range(2):
        arrive(scattered[p])
        total = precv[p, 0].astype(F32)
        for n in range(1, nx):
            total = total + precv[p, n].astype(F32)
        who = y if p == 0 else 1 - y
        ybuf[who, y] = total.astype(BF16)
        over += begin(
            [remote(ybuf.at[who, y], ybuf.at[who, y], y_s(p), place.partner())], sent
        )

    def chunk(slot):
        return lax.rem(slot + 1, nz)

    arrive(over)
    for p in range(2):
        total = ybuf[p, 0].astype(F32) + ybuf[p, 1].astype(F32)
        dw[p, chunk(z), x] = total.T.astype(BF16)

    one, two = y, 1 - y
    piece = dw.at[one, chunk(z), x]
    by_x = begin(
        [remote(piece, piece, ax_s(t - 1), place.at(x=place.other_x(t))) for t in range(1, nx)],
        sent,
    )
    piece = dw.at[two, chunk(z), x]
    by_z = begin(
        [remote(piece, piece, an_s(t - 1), place.along_z(t)) for t in range(1, nz)], sent
    )
    half = nx // 2
    wide = ring_z(
        place, lambda slot, part: dw.at[one, chunk(slot), pl.ds(part * half, half)], az_s, sent
    )
    passed = []

    def pass_on(t):
        piece = dw.at[two, chunk(lax.rem(z + nz - t, nz)), x]
        passed.extend(
            begin(
                [
                    remote(piece, piece, aw_s(t, n - 1), place.at(x=place.other_x(n)))
                    for n in range(1, nx)
                ],
                sent,
            )
        )

    near = [t for n in range(1, nz // 2) for t in (n, nz - n)] + [nz // 2]
    pass_on(0)
    for t in near[:2]:
        by_z[t - 1].wait_recv()
        pass_on(t)
    arrive(by_x)
    next(wide)
    for t in near[2:]:
        by_z[t - 1].wait_recv()
        pass_on(t)
    for _ in wide:
        pass
    arrive(returned)
    d_beta[pl.ds(1 - y, 1), :] = got_gate[0:1]
    d_lg[pl.ds(1 - y, 1), :] = got_gate[1:2]
    arrive(passed)
    for copy in sent:
        copy.wait_send()


def finish_kernel(*refs):
    ins, outs = refs[:6], refs[6:]
    for src, dst in zip(ins[:5], outs[:5]):
        dst[...] = src[...]
    heads, nz, nx = ins[5].shape[:3]
    for c in range(nz):
        for n in range(nx):
            for p in range(heads):
                rows = pl.ds((c * nx + n) * HD, HD)
                outs[5][rows, p * HD : (p + 1) * HD] = ins[5][p, c, n]


def vmem(count):
    return [pl.BlockSpec(memory_space=pltpu.VMEM)] * count


def shards(nx, nz, layer_input, q, k, v, beta, lg, do):
    sd = jax.ShapeDtypeStruct
    rows = sd((2, T), F32)
    wide = sd(q.shape, BF16)
    scratch = pltpu.VMEM
    sems = [
        (6,), (1,), (nz - 1,), (2, 2, nz // 2), (nx - 1,), (4,), (2, nz - 1), (2, nx - 1), (2,),
        (nx - 1,), (nz - 1,), (2, 2, nz // 2), (nz, nx - 1),
    ]
    outs = pl.pallas_call(
        lambda *refs: layer_kernel(nx, nz, *refs),
        out_shape=(wide, wide, wide, rows, rows, sd((2, nz, nx, HD, HD), BF16)),
        in_specs=[pl.BlockSpec(memory_space=pltpu.HBM)] * 7, out_specs=tuple(vmem(6)),
        scratch_shapes=[
            scratch((2, 4, T, HD), BF16), scratch((2, 2, 2, T), F32),
            scratch((nz, T, layer_input.shape[1]), BF16),
            scratch((2, T, T), F32), scratch((2, T, 2 * HD), F32), scratch((2, T, HD), F32),
            scratch((2, 3 * HD, HD), F32), scratch((nz, 3 * HD, HD), F32),
            scratch((2, 3 * HD, HD), F32), scratch((2, 3 * HD, HD), F32), scratch((3, 3 * HD, HD), F32),
            scratch((nx, 3 * HD, HD), F32), scratch((nx + 1, HD, HD), F32), scratch((nx + 1, HD, HD), F32),
            scratch((2, 2, HD, HD), F32),
            scratch((2, 2, T, HD), F32), scratch((2, 3, T, HD), BF16), scratch((2, 8, T), F32), scratch((8, T), F32),
            scratch((2, nz, T, HD), BF16), scratch((2, nx, HD, HD), BF16), scratch((2, nx, HD, HD), BF16),
            scratch((2, 2, HD, HD), BF16), pltpu.SemaphoreType.DMA((6,)),
        ]
        + [pltpu.SemaphoreType.DMA(shape) for shape in sems for _ in range(2)],
        compiler_params=pltpu.CompilerParams(
            collective_id=0, has_side_effects=True, vmem_limit_bytes=48 * 2**20
        ),
        name="layer",
    )(*(pltpu.with_memory_space_constraint(a, pltpu.HBM) for a in (layer_input, q, k, v, do, beta.T, lg.T)))
    dq, dk, dv, d_beta, d_lg, dw = pl.pallas_call(
        finish_kernel,
        out_shape=(wide, wide, wide, rows, rows, sd((nz * nx * HD, v.shape[1]), BF16)),
        in_specs=vmem(6), out_specs=tuple(vmem(6)),
        compiler_params=pltpu.CompilerParams(vmem_limit_bytes=12 * 2**20), name="finish",
    )(*outs)
    return dq, dk, dv, d_beta.T, d_lg.T, dw


def solution(mesh):
    nz = mesh.shape["head"]
    nx = mesh.shape["seq"] // (nz * NY)
    split = P("seq", "head")
    return jax.shard_map(
        lambda *args: shards(nx, nz, *args),
        mesh=mesh, in_specs=(split,) * 7, out_specs=(split,) * 5 + (P(None, "head"),),
        check_vma=False,
    )
```

```python
import jax
import jax.numpy as jnp
from jax import lax
from jax.experimental import pallas as pl
from jax.experimental.pallas import tpu as pltpu
from jax.sharding import PartitionSpec as P

HD = 128
T = 128
F32 = jnp.float32
BF16 = jnp.bfloat16
HIGHEST = lax.Precision.HIGHEST
NY = 2


def dot(a, b, ca=1, cb=0):
    return lax.dot_general(
        a, b, (((ca,), (cb,)), ((), ())), precision=HIGHEST, preferred_element_type=F32
    )


def dot_exact(a, b, ca=1, cb=0):
    return lax.dot_general(a, b, (((ca,), (cb,)), ((), ())), preferred_element_type=F32)


def iotas():
    return (
        lax.broadcasted_iota(jnp.int32, (T, T), 0),
        lax.broadcasted_iota(jnp.int32, (T, T), 1),
    )


def unit_inverse(strict_lower):
    line, col = iotas()
    same = (line >= 64) == (col >= 64)
    diag_part = jnp.where(same, strict_lower, 0.0)
    below = jnp.where(same, 0.0, strict_lower)
    inverse = jnp.where(line == col, 1.0, 0.0) - diag_part
    power = dot(diag_part, diag_part)
    covered = 4
    while covered < 64:
        both = dot(jnp.concatenate([power, inverse], 0), power)
        inverse = inverse + both[T:]
        power = both[:T]
        covered = covered * 2
    inverse = inverse + dot(inverse, power)
    return inverse - dot(dot(inverse, below), inverse)


def as_column(row):
    line, col = iotas()
    return jnp.sum(jnp.where(line == col, row, 0.0), axis=1, keepdims=True)


def as_row(column):
    line, col = iotas()
    return jnp.sum(jnp.where(line == col, column, 0.0), axis=0, keepdims=True)


def gate_parts(lg_row):
    line, col = iotas()
    run_col = jnp.sum(jnp.where(col <= line, lg_row, 0.0), axis=1, keepdims=True)
    run_row = as_row(run_col)
    total = jnp.sum(lg_row, axis=1, keepdims=True)
    causal = line >= col
    decay = jnp.where(causal, jnp.exp(jnp.where(causal, run_col - run_row, 0.0)), 0.0)
    return decay, jnp.exp(run_col), jnp.exp(total - run_col), jnp.exp(total)


def local_maps(q, k, v, do, beta_row, lg_row):
    line, col = iotas()
    beta = as_column(beta_row)
    decay, growth, tail, keep = gate_parts(lg_row)
    keys = k.astype(F32)
    scores = decay * dot_exact(q, k, 1, 1)
    lower = beta * jnp.where(line > col, decay * dot_exact(k, k, 1, 1), 0.0)
    inverse = unit_inverse(lower)
    uw = dot(inverse, jnp.concatenate([beta * v.astype(F32), (beta * growth) * keys], 1))
    back = dot(scores, do.astype(F32), 0, 0)
    bw = dot(tail * keys, uw, 0, 0)
    eye = jnp.where(line == col, 1.0, 0.0)
    a = keep * eye - bw[:, HD:]
    b = bw[:, :HD]
    c = dot(growth * q.astype(F32), do.astype(F32), 0, 0) - dot(uw[:, HD:], back, 0, 0)
    return (a, b, c), (inverse, uw, back)


def local_update(k, beta_row, lg_row, inverse, uw, back, state, adj):
    tail = gate_parts(lg_row)[2]
    update = uw[:, :HD] - dot(uw[:, HD:], state)
    e = dot(inverse, back + dot(tail * k.astype(F32), adj), 0, 0)
    return update, e, as_column(beta_row) * e


def local_grads(q, k, v, do, beta_row, lg_row, update, e, state, adj):
    line, col = iotas()
    beta = as_column(beta_row)
    decay, growth, tail, keep = gate_parts(lg_row)
    queries, keys, values, grads = (m.astype(F32) for m in (q, k, v, do))
    de = jnp.concatenate([grads, e], 0)
    by_state = dot(de, state, 1, 1)
    by_update = dot(de, update, 1, 1)
    nz = dot(update, adj, 1, 1)
    y = decay * by_update[:T]
    xp = -jnp.where(line > col, decay * by_update[T:], 0.0)
    by_key = dot(jnp.concatenate([xp, y], 0), keys)
    r = by_key[:T] - growth * by_state[T:]
    crossed = dot(
        jnp.concatenate([beta * xp, y], 0), jnp.concatenate([keys, queries], 0), 0, 0
    )
    dq = growth * by_state[:T] + by_key[T:]
    tail_nz = tail * nz
    dk_col = crossed + tail_nz
    dk_row = beta * r
    d_beta = jnp.sum(e * values + keys * r, axis=1, keepdims=True)
    d_run = jnp.sum(queries * dq + keys * (dk_row - dk_col), axis=1, keepdims=True)
    last = jnp.sum(tail_nz * keys, axis=(0, 1), keepdims=True) + keep * jnp.sum(
        adj * state, axis=(0, 1), keepdims=True
    )
    d_lg = jnp.sum(jnp.where(line >= col, d_run, 0.0), axis=0, keepdims=True) + last
    return dq, dk_row + dk_col, as_row(d_beta), d_lg


class Place:
    def __init__(self, nx, nz):
        s = lax.axis_index("seq")
        self.nx, self.nz = nx, nz
        self.x = s // (nz * NY)
        self.z = lax.rem(s // NY, nz)
        self.y = lax.rem(s, NY)
        self.h = lax.axis_index("head")

    def at(self, x=None, z=None, y=None):
        x = self.x if x is None else x
        z = self.z if z is None else z
        y = self.y if y is None else y
        return {"seq": (x * self.nz + z) * NY + y}

    def partner(self):
        return self.at(y=1 - self.y)

    def along_z(self, t):
        return self.at(z=lax.rem(self.z + t, self.nz))

    def other_x(self, t):
        return lax.rem(self.x + t, self.nx)

    def along_head(self, t):
        return {"head": lax.rem(self.h + t, self.nz)}

    def swap_to(self):
        return {**self.at(z=lax.rem(self.h + self.nz - 1, self.nz)), "head": self.z}

    def swap_from(self):
        return {**self.at(z=self.h), "head": lax.rem(self.z + 1, self.nz)}

    def greet(self):
        barrier = pltpu.get_barrier_semaphore()
        peers = [self.partner(), self.swap_to(), self.swap_from()]
        peers += [self.along_z(t) for t in range(1, self.nz)]
        peers += [self.along_head(t) for t in range(1, self.nz)]
        peers += [self.at(x=self.other_x(t)) for t in range(1, self.nx)]
        for peer in peers:
            pl.semaphore_signal(
                barrier, inc=1, device_id=peer, device_id_type=pl.DeviceIdType.MESH
            )
        pl.semaphore_wait(barrier, len(peers))


def remote(src, dst, sems, device):
    return pltpu.make_async_remote_copy(
        src_ref=src, dst_ref=dst, send_sem=sems[0], recv_sem=sems[1],
        device_id=device, device_id_type=pl.DeviceIdType.MESH,
    )


def begin(copies, sent):
    for copy in copies:
        copy.start()
    sent += copies
    return copies


def arrive(copies):
    for copy in copies:
        copy.wait_recv()


def ring_z(place, view, sems, sent):
    nz, z = place.nz, place.z
    steps = nz // 2
    before = {}
    for t in range(1, steps + 1):
        for part in range(2):
            for way, away, ahead in ((0, nz - t + 1, 1), (1, t - 1, nz - 1)):
                if (way, part) in before:
                    before.pop((way, part)).wait_recv()
                if t == steps and part != way:
                    continue
                src = view(lax.rem(z + away, nz), part)
                copy = remote(src, src, sems(way, part, t - 1), place.along_z(ahead))
                copy.start()
                sent.append(copy)
                before[way, part] = copy
        yield t
    arrive(before.values())


OFFSET, MAP, ADJ = slice(0, HD), slice(HD, 2 * HD), slice(2 * HD, 3 * HD)


def compose(out, later, earlier):
    a, below = later[MAP], earlier[MAP]
    ab = dot(a, jnp.concatenate([below, earlier[OFFSET]], 1))
    c = earlier[ADJ] + dot(below, later[ADJ], 0, 0)
    b = ab[:, HD:] + later[OFFSET]
    out[MAP] = ab[:, :HD]
    out[OFFSET] = b
    out[ADJ] = c


def chains(blocks, count, forth, aback):
    def step(n, carry):
        m = count - 1 - n
        forth[n + 1] = dot(blocks[n, MAP], forth[n]) + blocks[n, OFFSET]
        aback[m] = dot(blocks[m, MAP], aback[m + 1], 0, 0) + blocks[m, ADJ]
        return carry

    lax.fori_loop(0, count, step, 0)


def layer_kernel(
    nx, nz, li, q, k, v, do, beta, lg, dq, dk, dv, d_beta, d_lg, dw,
    inp, gates, xg, inverse, uw, back, pair, zbuf, left, right, joined, xbuf, xf, xb, both,
    written, ret, ret_gate, got_gate, g, psend, precv, ybuf, load_sems, *sem_refs
):
    in_s, sw_s, hd_s, z_s, x_s, ret_s, g_s, p_s, y_s, ax_s, an_s, az_s, aw_s = (
        (lambda a, b: lambda *i: (a.at[i], b.at[i]))(sem_refs[2 * n], sem_refs[2 * n + 1])
        for n in range(13)
    )
    place = Place(nx, nz)
    x, z, y, h = place.x, place.z, place.y, place.h
    mine = pl.ds(pl.multiple_of(y * HD, HD), HD)
    yours = pl.ds(pl.multiple_of((1 - y) * HD, HD), HD)
    sent = []
    loads = [
        pltpu.make_async_copy(ref.at[:, mine], inp.at[0, n], load_sems.at[n])
        for n, ref in enumerate((q, k, v, do))
    ]
    loads += [
        pltpu.make_async_copy(ref, gates.at[0, n], load_sems.at[4 + n])
        for n, ref in enumerate((beta, lg))
    ]
    for load in loads:
        load.start()
    place.greet()

    asked = [
        remote(ref.at[:, yours], inp.at[1, n], in_s(n), place.partner())
        for n, ref in enumerate((q, k, v, do))
    ]
    asked += [
        remote(ref, gates.at[1, n], in_s(4 + n), place.partner())
        for n, ref in enumerate((beta, lg))
    ]
    begin(asked, sent)
    swapped = begin([remote(li, xg.at[z], sw_s(0), place.swap_to())], sent)

    line, col = iotas()
    zero = jnp.zeros((HD, HD), F32)
    for ref in (left, right):
        for n in range(2):
            ref[n, MAP] = jnp.where(line == col, 1.0, 0.0)
            ref[n, OFFSET] = zero
            ref[n, ADJ] = zero
    xf[0] = zero
    xb[nx] = zero
    ret_gate[...] = jnp.zeros_like(ret_gate)
    for load in loads:
        load.wait()

    def inputs(n):
        return [inp[n, i] for i in range(4)] + [gates[n, i, pl.ds(y, 1), :] for i in range(2)]

    def maps_of(n, carry):
        @pl.when(n == 1)
        def _():
            arrive(asked)

        (a, b, c), (inv, u, f) = local_maps(*inputs(n))
        slot = lax.rem(y + n, 2)
        pair[slot, MAP] = a
        pair[slot, OFFSET] = b
        pair[slot, ADJ] = c
        inverse[n] = inv
        uw[n] = u
        back[n] = f
        return carry

    lax.fori_loop(0, 2, maps_of, 0)
    compose(zbuf.at[z], pair.at[1], pair.at[0])
    part_rows = 3 * HD // 2

    def zview(slot, part):
        return zbuf.at[slot, pl.ds(part * part_rows, part_rows)]

    def fold(t):
        wrapped = (z < t).astype(jnp.int32)
        acc = left.at[wrapped]
        compose(acc, acc, zbuf.at[lax.rem(z + nz - t, nz)])
        if t < nz // 2:
            wrapped = (z + t >= nz).astype(jnp.int32)
            acc = right.at[wrapped]
            compose(acc, zbuf.at[lax.rem(z + t, nz)], acc)

    for t in ring_z(place, zview, z_s, sent):
        if t > 1:
            fold(t - 1)
    arrive(swapped)
    spread = begin(
        [remote(xg.at[h], xg.at[h], hd_s(n - 1), place.along_head(n)) for n in range(1, nz)], sent
    )
    fold(nz // 2)
    compose(joined.at[0], left.at[0], right.at[1])
    compose(joined.at[1], left.at[1], right.at[0])
    compose(joined.at[2], zbuf.at[z], joined.at[0])
    compose(xbuf.at[x], joined.at[1], joined.at[2])
    totals = []
    for t in range(1, nx):
        other = place.other_x(t)
        low = jnp.where(other > x, 0, HD)
        rows = xbuf.at[x, pl.ds(pl.multiple_of(low, HD), 2 * HD)]
        totals.append(remote(rows, rows, x_s(t - 1), place.at(x=other)))
    begin(totals, sent)
    arrive(totals)
    chains(xbuf, nx, xf, xb)
    state = dot(joined[0, MAP], xf[x]) + joined[0, OFFSET]
    adj = dot(joined[1, MAP], xb[x + 1], 0, 0) + joined[1, ADJ]
    both[0, 0] = state
    both[0, 1] = dot(pair[1, MAP], adj, 0, 0) + pair[1, ADJ]
    both[1, 0] = dot(pair[0, MAP], state) + pair[0, OFFSET]
    both[1, 1] = adj

    given = [remote(ret.at[1, 2], g.at[1, z], ret_s(2), place.partner())]
    returned = [
        remote(ret.at[1, 0], dq.at[:, mine], ret_s(0), place.partner()),
        remote(ret.at[1, 1], dk.at[:, mine], ret_s(1), place.partner()),
        remote(ret_gate.at[1], got_gate, ret_s(3), place.partner()),
    ]

    def update_of(turn, carry):
        n = 1 - turn
        slot = lax.rem(y + n, 2)
        parts = inputs(n)
        update, e, gv = local_update(
            parts[1], parts[4], parts[5], inverse[n], uw[n], back[n], both[slot, 0], both[slot, 1]
        )
        written[n, 0] = update
        written[n, 1] = e
        ret[n, 2] = gv.astype(BF16)

        @pl.when(turn == 0)
        def _():
            for copy in given:
                copy.start()

        return carry

    def grads_of(turn, carry):
        n = 1 - turn
        slot = lax.rem(y + n, 2)
        gq, gk, gb, gl = local_grads(
            *inputs(n), written[n, 0], written[n, 1], both[slot, 0], both[slot, 1]
        )
        ret[n, 0] = gq.astype(BF16)
        ret[n, 1] = gk.astype(BF16)
        ret_gate[n, 0:1] = gb
        ret_gate[n, 1:2] = gl

        @pl.when(turn == 0)
        def _():
            for copy in returned:
                copy.start()

        return carry

    def share(p):
        return begin(
            [
                remote(g.at[p, z], g.at[p, z], g_s(p, t - 1), place.along_z(t))
                for t in range(1, nz)
            ],
            sent,
        )

    lax.fori_loop(0, 2, update_of, 0)
    g[0, z] = ret[0, 2]
    shared = [share(0)]
    lax.fori_loop(0, 2, grads_of, 0)
    sent += given + returned
    arrive(given)
    shared.append(share(1))
    dq[:, mine] = ret[0, 0]
    dk[:, mine] = ret[0, 1]
    dv[:, mine] = ret[0, 2]
    dv[:, yours] = g[1, z]
    d_beta[pl.ds(y, 1), :] = ret_gate[0, 0:1]
    d_lg[pl.ds(y, 1), :] = ret_gate[0, 1:2]

    arrive(spread)
    scattered = []
    for p in range(2):
        arrive(shared[p])
        feats = xg[...].reshape(nz * T, xg.shape[2])
        total = dot_exact(g[p].reshape(nz * T, HD), feats, 0, 0)
        for n in range(nx):
            psend[p, n] = total[:, n * HD : (n + 1) * HD].astype(BF16)
        scattered.append(
            begin(
                [
                    remote(
                        psend.at[p, place.other_x(t)], precv.at[p, x], p_s(p, t - 1),
                        place.at(x=place.other_x(t)),
                    )
                    for t in range(1, nx)
                ],
                sent,
            )
        )
        precv[p, x] = psend[p, x]
    over = []
    for p in range(2):
        arrive(scattered[p])
        total = precv[p, 0].astype(F32)
        for n in range(1, nx):
            total = total + precv[p, n].astype(F32)
        who = y if p == 0 else 1 - y
        ybuf[who, y] = total.astype(BF16)
        over += begin(
            [remote(ybuf.at[who, y], ybuf.at[who, y], y_s(p), place.partner())], sent
        )

    def chunk(slot):
        return lax.rem(slot + 1, nz)

    arrive(over)
    for p in range(2):
        total = ybuf[p, 0].astype(F32) + ybuf[p, 1].astype(F32)
        dw[p, chunk(z), x] = total.T.astype(BF16)

    one, two = y, 1 - y
    piece = dw.at[one, chunk(z), x]
    by_x = begin(
        [remote(piece, piece, ax_s(t - 1), place.at(x=place.other_x(t))) for t in range(1, nx)],
        sent,
    )
    piece = dw.at[two, chunk(z), x]
    by_z = begin(
        [remote(piece, piece, an_s(t - 1), place.along_z(t)) for t in range(1, nz)], sent
    )
    half = nx // 2
    wide = ring_z(
        place, lambda slot, part: dw.at[one, chunk(slot), pl.ds(part * half, half)], az_s, sent
    )
    passed = []

    def pass_on(t):
        piece = dw.at[two, chunk(lax.rem(z + nz - t, nz)), x]
        passed.extend(
            begin(
                [
                    remote(piece, piece, aw_s(t, n - 1), place.at(x=place.other_x(n)))
                    for n in range(1, nx)
                ],
                sent,
            )
        )

    near = [t for n in range(1, nz // 2) for t in (n, nz - n)] + [nz // 2]
    pass_on(0)
    for t in near[:2]:
        by_z[t - 1].wait_recv()
        pass_on(t)
    arrive(by_x)
    next(wide)
    for t in near[2:]:
        by_z[t - 1].wait_recv()
        pass_on(t)
    for _ in wide:
        pass
    arrive(returned)
    d_beta[pl.ds(1 - y, 1), :] = got_gate[0:1]
    d_lg[pl.ds(1 - y, 1), :] = got_gate[1:2]
    arrive(passed)
    for copy in sent:
        copy.wait_send()


def finish_kernel(*refs):
    ins, outs = refs[:6], refs[6:]
    for src, dst in zip(ins[:5], outs[:5]):
        dst[...] = src[...]
    heads, nz, nx = ins[5].shape[:3]
    for c in range(nz):
        for n in range(nx):
            for p in range(heads):
                rows = pl.ds((c * nx + n) * HD, HD)
                outs[5][rows, p * HD : (p + 1) * HD] = ins[5][p, c, n]


def vmem(count):
    return [pl.BlockSpec(memory_space=pltpu.VMEM)] * count


def shards(nx, nz, layer_input, q, k, v, beta, lg, do):
    sd = jax.ShapeDtypeStruct
    rows = sd((2, T), F32)
    wide = sd(q.shape, BF16)
    scratch = pltpu.VMEM
    sems = [
        (6,), (1,), (nz - 1,), (2, 2, nz // 2), (nx - 1,), (4,), (2, nz - 1), (2, nx - 1), (2,),
        (nx - 1,), (nz - 1,), (2, 2, nz // 2), (nz, nx - 1),
    ]
    outs = pl.pallas_call(
        lambda *refs: layer_kernel(nx, nz, *refs),
        out_shape=(wide, wide, wide, rows, rows, sd((2, nz, nx, HD, HD), BF16)),
        in_specs=[pl.BlockSpec(memory_space=pltpu.HBM)] * 7, out_specs=tuple(vmem(6)),
        scratch_shapes=[
            scratch((2, 4, T, HD), BF16), scratch((2, 2, 2, T), F32),
            scratch((nz, T, layer_input.shape[1]), BF16),
            scratch((2, T, T), F32), scratch((2, T, 2 * HD), F32), scratch((2, T, HD), F32),
            scratch((2, 3 * HD, HD), F32), scratch((nz, 3 * HD, HD), F32),
            scratch((2, 3 * HD, HD), F32), scratch((2, 3 * HD, HD), F32), scratch((3, 3 * HD, HD), F32),
            scratch((nx, 3 * HD, HD), F32), scratch((nx + 1, HD, HD), F32), scratch((nx + 1, HD, HD), F32),
            scratch((2, 2, HD, HD), F32),
            scratch((2, 2, T, HD), F32), scratch((2, 3, T, HD), BF16), scratch((2, 8, T), F32), scratch((8, T), F32),
            scratch((2, nz, T, HD), BF16), scratch((2, nx, HD, HD), BF16), scratch((2, nx, HD, HD), BF16),
            scratch((2, 2, HD, HD), BF16), pltpu.SemaphoreType.DMA((6,)),
        ]
        + [pltpu.SemaphoreType.DMA(shape) for shape in sems for _ in range(2)],
        compiler_params=pltpu.CompilerParams(
            collective_id=0, has_side_effects=True, vmem_limit_bytes=48 * 2**20
        ),
        name="layer",
    )(*(pltpu.with_memory_space_constraint(a, pltpu.HBM) for a in (layer_input, q, k, v, do, beta.T, lg.T)))
    dq, dk, dv, d_beta, d_lg, dw = pl.pallas_call(
        finish_kernel,
        out_shape=(wide, wide, wide, rows, rows, sd((nz * nx * HD, v.shape[1]), BF16)),
        in_specs=vmem(6), out_specs=tuple(vmem(6)),
        compiler_params=pltpu.CompilerParams(vmem_limit_bytes=12 * 2**20), name="finish",
    )(*outs)
    return dq, dk, dv, d_beta.T, d_lg.T, dw


def solution(mesh):
    nz = mesh.shape["head"]
    nx = mesh.shape["seq"] // (nz * NY)
    split = P("seq", "head")
    return jax.shard_map(
        lambda *args: shards(nx, nz, *args),
        mesh=mesh, in_specs=(split,) * 7, out_specs=(split,) * 5 + (P(None, "head"),),
        check_vma=False,
    )
```
